1024 devices in a mesh: dp: 64 (over z_lo, y, core), vox: 16 (over z_hi, x).
Axes of the slice: x: 4, y: 8, z: 16 (z_hi: 4, z_lo: 4; z = z_hi * 4 + z_lo), core: 2. Of those that a mesh axis runs over, the one named last changes fastest.
Arguments:
- kernels: bfloat16 [3072, 65536], P('dp', 'vox'), may hold values from -0.0234375 to 0.0234375
- observed: float32 [8, 3072], P(None, 'dp'), may hold values from -6 to 6
- initial: float32 [8, 65536], P(None, 'vox'), may hold values from -6 to 6
- threshold: float32 [8, 16, 2], replicated, may hold values from 0.05 to 0.5
Outputs:
- coefficients: float32 [8, 65536], P(None, 'vox')
- residual: float32 [8, 3072], P(None, 'dp')
The draws below stay inside these ranges and needn't reach their ends.
All inputs are finite; a program needn't handle non-finite values.
Results may differ from the reference program's by a relative error of at most 0.0043.
Values may be sent and summed in bfloat16 or wider, within the bound.
A program may use at most 32 MiB of HBM per device.

```python
import math
import jax
import jax.numpy as jnp
from jax import lax

LAYERS = 16
CELLS_DEV = 256
MODELS = 8
ITERS = 2
VOXELS = 65536
ROWS = 3072
N_VOX = 16


def level_of(key, dims, cuts, least, top_value):
    def one(dim, shards_of):
        draws = jax.random.uniform(jax.random.fold_in(jax.random.fold_in(key, 6), dim), (shards_of,), jnp.float32, least / len(cuts), top_value / len(cuts))
        return jnp.repeat(jnp.exp(draws), dims[dim] // shards_of).reshape((-1,) + (1,) * (len(dims) - dim - 1))

    level = one(*cuts[0])
    for cut in cuts[1:]:
        level = level * one(*cut)
    return level


def scatter_about(key, dims, width, reach, pieces=(), kind=jnp.bfloat16):
    array = width * jax.random.normal(key, dims, jnp.float32)
    if pieces:
        array = array * level_of(key, dims, pieces, -0.22, 0.18)
    return jnp.clip(array, -reach, reach).astype(kind)


def setup_inputs(seed: int = 0) -> dict:
    splits = jax.random.split(jax.random.key(seed), 5)
    kernels = scatter_about(splits[0], (ROWS, VOXELS), VOXELS ** -0.5, 0.0234375, ((0, 64), (1, 16)))
    observed = scatter_about(splits[1], (MODELS, ROWS), 1.0, 6.0, ((1, 64),), jnp.float32)
    initial = scatter_about(splits[2], (MODELS, VOXELS), 1.0, 6.0, ((1, 16),), jnp.float32)
    threshold = jnp.clip(jnp.exp(jax.random.uniform(splits[3], (MODELS, LAYERS, 2), jnp.float32, math.log(0.05), math.log(0.5))), 0.05, 0.5)
    return dict(kernels=kernels, observed=observed, initial=initial, threshold=threshold)


step_size = 0.5


def to_curve(flat_model):
    models_count = flat_model.shape[0]
    half_cells = CELLS_DEV // 2
    arranged = flat_model.reshape(models_count, N_VOX, LAYERS, 2, half_cells)
    arranged = jnp.transpose(arranged, (0, 2, 3, 1, 4))
    return arranged.reshape(models_count, LAYERS, 2, N_VOX * half_cells)


def from_curve(arranged):
    models_count = arranged.shape[0]
    half_cells = CELLS_DEV // 2
    spread = arranged.reshape(models_count, LAYERS, 2, N_VOX, half_cells)
    spread = jnp.transpose(spread, (0, 3, 1, 2, 4))
    return spread.reshape(models_count, N_VOX * LAYERS * CELLS_DEV)


def forward_wave(arranged):
    even_part = arranged[:, :, 0, :]
    odd_part = arranged[:, :, 1, :]
    detail = odd_part - 0.5 * (even_part + jnp.roll(even_part, -1, axis=-1))
    smooth = even_part + 0.25 * (jnp.roll(detail, 1, axis=-1) + detail)
    return jnp.stack([smooth, detail], axis=2)


def inverse_wave(arranged):
    smooth = arranged[:, :, 0, :]
    detail = arranged[:, :, 1, :]
    even_part = smooth - 0.25 * (jnp.roll(detail, 1, axis=-1) + detail)
    odd_part = detail + 0.5 * (even_part + jnp.roll(even_part, -1, axis=-1))
    return jnp.stack([even_part, odd_part], axis=2)


def shrink(values, thresholds):
    return jnp.sign(values) * jnp.maximum(jnp.abs(values) - thresholds, 0.0)


def reference(kernels, observed, initial, threshold):
    thresholds = threshold[:, :, :, None]
    wavelets = to_curve(initial)
    voxel_model = from_curve(inverse_wave(wavelets)).astype(jnp.bfloat16)
    residual = observed
    for iteration in range(ITERS):
        predicted = lax.dot_general(voxel_model, kernels, (((1,), (1,)), ((), ())), preferred_element_type=jnp.float32)
        residual = observed - predicted
        gradient = jnp.dot(residual.astype(jnp.bfloat16), kernels, preferred_element_type=jnp.float32)
        updated = wavelets + step_size * forward_wave(to_curve(gradient))
        wavelets = shrink(updated, thresholds)
        if iteration + 1 < ITERS:
            voxel_model = from_curve(inverse_wave(wavelets)).astype(jnp.bfloat16)
    return from_curve(wavelets), residual
```

```python
import functools

import jax
import jax.numpy as jnp
from jax import lax
from jax.experimental import pallas as pl
from jax.experimental.pallas import tpu as pltpu
from jax.sharding import PartitionSpec as P

MESH = pl.DeviceIdType.MESH
F32 = jnp.float32
BF16 = jnp.bfloat16
LANES = 128
LAYERS = 16
SLOTS = 8

NC, NY, NZ, NV = 2, 8, 4, 16


def lane_of(rows=8):
    return lax.broadcasted_iota(jnp.int32, (rows, LANES), 1)


def shrink(values, cutoff):
    return jnp.where(
        values > cutoff, values - cutoff, jnp.where(values < -cutoff, values + cutoff, 0.0)
    )


def take_prev(tile, edge):
    return jnp.where(lane_of() == 0, edge, pltpu.roll(tile, 1, 1))


def take_next(tile, edge):
    return jnp.where(lane_of() == LANES - 1, edge, pltpu.roll(tile, LANES - 1, 1))


def inverse_wave(smooth, detail, detail_before, smooth_after, detail_after):
    even = smooth - 0.25 * (take_prev(detail, detail_before) + detail)
    even_after = smooth_after - 0.25 * (detail[:, LANES - 1 :] + detail_after)
    odd = detail + 0.5 * (even + take_next(even, even_after))
    return even, odd


def rows_dot(a, b):
    return lax.dot_general(a, b, (((1,), (1,)), ((), ())), preferred_element_type=F32)


def kernel(
    sizes,
    k_ref,
    obs_ref,
    init_ref,
    thr_ref,
    coef_ref,
    resid_ref,
    pack,
    packs,
    edge_f32,
    edge,
    edges,
    model,
    pred_pad,
    pred_send,
    preds,
    stage,
    parts,
    sums_send,
    sums,
    chunks,
    finals,
    send_sem,
    recv_sem,
):
    nc, ny, nz, nv = sizes
    groups = nc * nz
    per = LAYERS // groups
    width = per * 2 * LANES
    rows = k_ref.shape[0]
    dp = lax.axis_index("dp")
    vox = lax.axis_index("vox")
    core = lax.rem(dp, nc)
    y = lax.rem(lax.div(dp, nc), ny)
    z = lax.div(dp, nc * ny)
    g = z * nc + core

    def vox_peer(k):
        return dp, lax.rem(vox + k, nv)

    def group_peer(k):
        other = lax.rem(g + k, groups)
        return (lax.div(other, nc) * ny + y) * nc + lax.rem(other, nc), vox

    def y_peer(k):
        return (z * ny + lax.rem(y + k, ny)) * nc + core, vox

    barrier = pltpu.get_barrier_semaphore()

    def greet(peer, count):
        def one(k, carry):
            pl.semaphore_signal(barrier, inc=1, device_id=peer(k), device_id_type=MESH)
            return carry

        lax.fori_loop(1, count, one, 0)

    greet(vox_peer, nv)
    greet(group_peer, groups)
    greet(y_peer, ny)

    def send(src, dst, phase, device):
        pltpu.make_async_remote_copy(
            src_ref=src,
            dst_ref=dst,
            send_sem=send_sem.at[phase],
            recv_sem=recv_sem.at[phase],
            device_id=device,
            device_id_type=MESH,
        ).start()

    def wait(ref, sem, phase):
        pltpu.make_async_copy(ref, ref, sem.at[phase]).wait()

    lane = lane_of()
    packed = jnp.zeros((8, LANES), F32)
    for layer in range(LAYERS):
        base = layer * 2 * LANES
        smooth = init_ref[:, base : base + LANES]
        detail = init_ref[:, base + LANES : base + 2 * LANES]
        at = layer * SLOTS
        if at:
            packed = jnp.where(lane == at, pltpu.roll(smooth, at, 1), packed)
        else:
            packed = jnp.where(lane == at, smooth, packed)
        packed = jnp.where(lane == at + 1, pltpu.roll(detail, at + 1, 1), packed)
        packed = jnp.where(lane == at + 4, pltpu.roll(detail, at + 5, 1), packed)
    pack[...] = packed
    slot = lax.broadcasted_iota(jnp.int32, (SLOTS, 2 * LANES), 0)
    column = lax.broadcasted_iota(jnp.int32, (SLOTS, 2 * LANES), 1)
    picked = (
        ((slot == 0) & (column == 0))
        | ((slot == 1) & (column == LANES))
        | ((slot == 2) & (column == 1))
        | ((slot == 3) & (column == LANES - 1))
        | ((slot == 4) & (column == 2 * LANES - 1))
    )
    pick = jnp.where(picked, 1.0, 0.0).astype(BF16)
    edge_f32[...] = jnp.zeros_like(edge_f32)
    pred_pad[...] = jnp.zeros_like(pred_pad)
    for layer in range(LAYERS):
        base = layer * 2 * LANES
        edge_f32[layer * SLOTS : (layer + 1) * SLOTS, 0:rows] = rows_dot(
            pick, k_ref[:, base : base + 2 * LANES]
        )
    edge[...] = edge_f32[...].astype(BF16)

    pl.semaphore_wait(barrier, (nv - 1) + (groups - 1) + (ny - 1))

    send(pack, packs.at[0], 0, vox_peer(nv - 1))
    send(pack, packs.at[1], 0, vox_peer(1))
    send(edge, edges.at[0], 1, vox_peer(nv - 1))
    send(edge, edges.at[1], 1, vox_peer(1))

    wait(packs, recv_sem, 0)
    after = packs[0]
    before = packs[1]
    for layer in range(LAYERS):
        base = layer * 2 * LANES
        at = layer * SLOTS
        even, odd = inverse_wave(
            init_ref[:, base : base + LANES],
            init_ref[:, base + LANES : base + 2 * LANES],
            before[:, at + 4 : at + 5],
            after[:, at : at + 1],
            after[:, at + 1 : at + 2],
        )
        model[:, base : base + LANES] = even.astype(BF16)
        model[:, base + LANES : base + 2 * LANES] = odd.astype(BF16)
    pred = rows_dot(model[...], k_ref[...])

    mine = pl.ds(pl.multiple_of(g * width, width), width)
    back = lax.rem(LANES - g * (per * SLOTS), LANES)
    after = pltpu.roll(after, back, 1)
    before = pltpu.roll(before, back, 1)
    pred_pad[:, 64:80] = thr_ref[:, 0, :]
    pred_pad[:, 96:112] = thr_ref[:, 1, :]
    cutoffs = pltpu.roll(pred_pad[...], lax.rem(LANES - g * per, LANES), 1)
    own = init_ref[:, mine]
    state = []
    for i in range(per):
        base = i * 2 * LANES
        at = i * SLOTS
        state.append(
            (
                own[:, base : base + LANES],
                own[:, base + LANES : base + 2 * LANES],
                before[:, at + 4 : at + 5],
                after[:, at : at + 1],
                after[:, at + 1 : at + 2],
            )
        )

    for it in range(2):
        phase = 2 + 4 * it
        pred_pad[:, 0:rows] = pred
        padded = jnp.where(lane < rows, pred_pad[...], 0.0)
        shared = padded[0:4] + pltpu.roll(padded[4:8], rows, 1)
        pred_send[it] = shared
        preds[it, vox] = shared

        def send_pred(k, carry):
            send(pred_send.at[it], preds.at[it, vox], phase, vox_peer(k))
            return carry

        lax.fori_loop(1, nv, send_pred, 0)
        wait(preds.at[it, pl.ds(0, nv - 1)], recv_sem, phase)
        total = preds[it, 0]
        for j in range(1, nv):
            total = total + preds[it, j]
        predicted = jnp.concatenate(
            [total[:, 0:rows], pltpu.roll(total, LANES - rows, 1)[:, 0:rows]], axis=0
        )
        residual = obs_ref[...] - predicted
        sent = residual.astype(BF16)

        if it == 0:
            wait(edges, recv_sem, 1)
            place = lax.rem(
                lax.broadcasted_iota(jnp.int32, (LAYERS * SLOTS, LANES), 0), SLOTS
            )
            edge_f32[...] = jnp.where(
                place < 3, edges[0].astype(F32), edges[1].astype(F32)
            )
        else:
            resid_ref[...] = residual
        grad = jnp.dot(sent, k_ref[...], preferred_element_type=F32).astype(BF16)
        edge_grad = rows_dot(sent, edge_f32[:, 0:rows].astype(BF16)).astype(BF16)
        for i in range(groups):
            stage[it, i, :, 0:width] = grad[:, i * width : (i + 1) * width]
            stage[it, i, :, width:] = edge_grad

        def send_part(k, carry):
            other = lax.rem(g + k, groups)
            send(stage.at[it, other], parts.at[it, k - 1], phase + 1, group_peer(k))
            return carry

        lax.fori_loop(1, groups, send_part, 0)
        wait(parts.at[it], recv_sem, phase + 1)
        total = stage[it, g].astype(F32)
        for i in range(groups - 1):
            total = total + parts[it, i].astype(F32)
        total = total.astype(BF16)
        sums_send[it] = total
        sums[it, y] = total

        def send_sum(k, carry):
            send(sums_send.at[it], sums.at[it, y], phase + 2, y_peer(k))
            return carry

        lax.fori_loop(1, ny, send_sum, 0)
        wait(sums.at[it, pl.ds(0, ny - 1)], recv_sem, phase + 2)
        total = sums[it, 0].astype(F32)
        for i in range(1, ny):
            total = total + sums[it, i].astype(F32)
        beside = pltpu.roll(total[:, width:], back, 1)

        for i in range(per):
            base = i * 2 * LANES
            at = i * SLOTS
            even = total[:, base : base + LANES]
            odd = total[:, base + LANES : base + 2 * LANES]
            even_after = beside[:, at : at + 1]
            odd_after = beside[:, at + 1 : at + 2]
            even_after2 = beside[:, at + 2 : at + 3]
            even_before = beside[:, at + 3 : at + 4]
            odd_before = beside[:, at + 4 : at + 5]
            detail = odd - 0.5 * (even + take_next(even, even_after))
            detail_before = odd_before - 0.5 * (even_before + even[:, 0:1])
            smooth = even + 0.25 * (take_prev(detail, detail_before) + detail)
            cut_s = cutoffs[:, 64 + i : 65 + i]
            cut_d = cutoffs[:, 96 + i : 97 + i]
            w_s, w_d, w_db, w_sa, w_da = state[i]
            w_s = shrink(w_s + 0.5 * smooth, cut_s)
            w_d = shrink(w_d + 0.5 * detail, cut_d)
            if it == 0:
                detail_after = odd_after - 0.5 * (even_after + even_after2)
                smooth_after = even_after + 0.25 * (detail[:, LANES - 1 :] + detail_after)
                w_db = shrink(w_db + 0.5 * detail_before, cut_d)
                w_sa = shrink(w_sa + 0.5 * smooth_after, cut_s)
                w_da = shrink(w_da + 0.5 * detail_after, cut_d)
                state[i] = (w_s, w_d, w_db, w_sa, w_da)
                even, odd = inverse_wave(w_s, w_d, w_db, w_sa, w_da)
                chunks[g, :, base : base + LANES] = even.astype(BF16)
                chunks[g, :, base + LANES : base + 2 * LANES] = odd.astype(BF16)
            else:
                finals[g, :, base : base + LANES] = w_s
                finals[g, :, base + LANES : base + 2 * LANES] = w_d

        target = chunks if it == 0 else finals

        def send_chunk(k, carry):
            send(target.at[g], target.at[g], phase + 3, group_peer(k))
            return carry

        lax.fori_loop(1, groups, send_chunk, 0)
        wait(target.at[pl.ds(0, groups - 1)], recv_sem, phase + 3)
        if it == 0:
            pred = rows_dot(chunks[0], k_ref[:, 0:width])
            for i in range(1, groups):
                pred = pred + rows_dot(chunks[i], k_ref[:, i * width : (i + 1) * width])
        else:
            for i in range(groups):
                coef_ref[:, i * width : (i + 1) * width] = finals[i]

    wait(packs, send_sem, 0)
    wait(edges, send_sem, 1)
    for it in range(2):
        phase = 2 + 4 * it
        target = chunks if it == 0 else finals
        wait(preds.at[it, pl.ds(0, nv - 1)], send_sem, phase)
        wait(parts.at[it], send_sem, phase + 1)
        wait(sums.at[it, pl.ds(0, ny - 1)], send_sem, phase + 2)
        wait(target.at[pl.ds(0, groups - 1)], send_sem, phase + 3)


def body(sizes, kernels, observed, initial, threshold):
    nc, ny, nz, nv = sizes
    groups = nc * nz
    width = (LAYERS // groups) * 2 * LANES
    vmem = pl.BlockSpec(memory_space=pltpu.VMEM)
    wide = width + LANES
    return pl.pallas_call(
        functools.partial(kernel, sizes),
        out_shape=(
            jax.ShapeDtypeStruct(initial.shape, F32),
            jax.ShapeDtypeStruct(observed.shape, F32),
        ),
        in_specs=[vmem] * 4,
        out_specs=(vmem, vmem),
        scratch_shapes=[
            pltpu.VMEM((8, LANES), F32),
            pltpu.VMEM((2, 8, LANES), F32),
            pltpu.VMEM((LAYERS * SLOTS, LANES), F32),
            pltpu.VMEM((LAYERS * SLOTS, LANES), BF16),
            pltpu.VMEM((2, LAYERS * SLOTS, LANES), BF16),
            pltpu.VMEM(initial.shape, BF16),
            pltpu.VMEM((8, LANES), F32),
            pltpu.VMEM((2, 4, LANES), F32),
            pltpu.VMEM((2, nv, 4, LANES), F32),
            pltpu.VMEM((2, groups, 8, wide), BF16),
            pltpu.VMEM((2, groups - 1, 8, wide), BF16),
            pltpu.VMEM((2, 8, wide), BF16),
            pltpu.VMEM((2, ny, 8, wide), BF16),
            pltpu.VMEM((groups, 8, width), BF16),
            pltpu.VMEM((groups, 8, width), F32),
            pltpu.SemaphoreType.DMA((10,)),
            pltpu.SemaphoreType.DMA((10,)),
        ],
        compiler_params=pltpu.CompilerParams(collective_id=0, has_side_effects=True),
    )(kernels, observed, initial, jnp.transpose(threshold, (0, 2, 1)))


def build(mesh, sizes):
    return jax.shard_map(
        functools.partial(body, sizes),
        mesh=mesh,
        in_specs=(P("dp", "vox"), P(None, "dp"), P(None, "vox"), P()),
        out_specs=(P(None, "vox"), P(None, "dp")),
        check_vma=False,
    )


def solution(mesh):
    return build(mesh, (NC, NY, NZ, NV))
```

```python
import functools

import jax
import jax.numpy as jnp
from jax import lax
from jax.experimental import pallas as pl
from jax.experimental.pallas import tpu as pltpu
from jax.sharding import PartitionSpec as P

MESH = pl.DeviceIdType.MESH
F32 = jnp.float32
BF16 = jnp.bfloat16
LANES = 128
LAYERS = 16
SLOTS = 8

NC, NY, NZ, NV = 2, 8, 4, 16


def lane_of(rows=8):
    return lax.broadcasted_iota(jnp.int32, (rows, LANES), 1)


def shrink(values, cutoff):
    return jnp.where(
        values > cutoff, values - cutoff, jnp.where(values < -cutoff, values + cutoff, 0.0)
    )


def take_prev(tile, edge):
    return jnp.where(lane_of() == 0, edge, pltpu.roll(tile, 1, 1))


def take_next(tile, edge):
    return jnp.where(lane_of() == LANES - 1, edge, pltpu.roll(tile, LANES - 1, 1))


def inverse_wave(smooth, detail, detail_before, smooth_after, detail_after):
    even = smooth - 0.25 * (take_prev(detail, detail_before) + detail)
    even_after = smooth_after - 0.25 * (detail[:, LANES - 1 :] + detail_after)
    odd = detail + 0.5 * (even + take_next(even, even_after))
    return even, odd


def rows_dot(a, b):
    return lax.dot_general(a, b, (((1,), (1,)), ((), ())), preferred_element_type=F32)


def kernel(
    sizes,
    k_hbm,
    obs_hbm,
    init_hbm,
    thr_hbm,
    coef_ref,
    resid_ref,
    k_ref,
    obs_ref,
    init_ref,
    thr_ref,
    pack,
    packs,
    edge_f32,
    edge,
    edges,
    model,
    pred_pad,
    pred_send,
    preds,
    stage,
    parts,
    sums_send,
    sums,
    chunks,
    finals,
    load_sem,
    send_sem,
    recv_sem,
):
    nc, ny, nz, nv = sizes
    groups = nc * nz
    per = LAYERS // groups
    width = per * 2 * LANES
    rows = k_ref.shape[0]
    dp = lax.axis_index("dp")
    vox = lax.axis_index("vox")
    core = lax.rem(dp, nc)
    y = lax.rem(lax.div(dp, nc), ny)
    z = lax.div(dp, nc * ny)
    g = z * nc + core

    loads = [
        pltpu.make_async_copy(init_hbm, init_ref, load_sem.at[0]),
        pltpu.make_async_copy(k_hbm, k_ref, load_sem.at[1]),
        pltpu.make_async_copy(obs_hbm, obs_ref, load_sem.at[2]),
        pltpu.make_async_copy(thr_hbm, thr_ref, load_sem.at[3]),
    ]
    for load in loads:
        load.start()

    def vox_peer(k):
        return dp, lax.rem(vox + k, nv)

    def group_peer(k):
        other = lax.rem(g + k, groups)
        return (lax.div(other, nc) * ny + y) * nc + lax.rem(other, nc), vox

    def y_peer(k):
        return (z * ny + lax.rem(y + k, ny)) * nc + core, vox

    vox_order = sorted(range(1, nv), key=lambda k: -min(k, nv - k))
    y_order = sorted(range(1, ny), key=lambda k: -min(k, ny - k))

    barrier = pltpu.get_barrier_semaphore()

    def greet(peer, k):
        pl.semaphore_signal(barrier, inc=1, device_id=peer(k), device_id_type=MESH)

    for k in vox_order:
        greet(vox_peer, k)
    for k in y_order:
        greet(y_peer, k)
    for k in range(1, groups):
        greet(group_peer, k)

    def send(src, dst, phase, device):
        pltpu.make_async_remote_copy(
            src_ref=src,
            dst_ref=dst,
            send_sem=send_sem.at[phase],
            recv_sem=recv_sem.at[phase],
            device_id=device,
            device_id_type=MESH,
        ).start()

    def wait(ref, sem, phase):
        pltpu.make_async_copy(ref, ref, sem.at[phase]).wait()

    def turn(tile, by):
        by = by % LANES
        return pltpu.roll(tile, by, 1) if by else tile

    lane = lane_of()
    slot = lax.rem(lane, SLOTS)
    loads[0].wait()
    packed = jnp.zeros((8, LANES), F32)
    for layer in range(LAYERS):
        base = layer * 2 * LANES
        smooth = init_ref[:, base : base + LANES]
        detail = init_ref[:, base + LANES : base + 2 * LANES]
        at = layer * SLOTS
        packed = jnp.where(lane == at, turn(smooth, at), packed)
        packed = jnp.where(lane == at + 1, turn(detail, at + 1), packed)
        packed = jnp.where(lane == at + 4, turn(detail, at + 5), packed)
    pack[...] = packed

    pl.semaphore_wait(barrier, (nv - 1) + (groups - 1) + (ny - 1))

    send(pack, packs.at[0], 0, vox_peer(nv - 1))
    send(pack, packs.at[1], 0, vox_peer(1))

    loads[1].wait()
    pick_slot = lax.broadcasted_iota(jnp.int32, (SLOTS, 2 * LANES), 0)
    column = lax.broadcasted_iota(jnp.int32, (SLOTS, 2 * LANES), 1)
    picked = (
        ((pick_slot == 0) & (column == 0))
        | ((pick_slot == 1) & (column == LANES))
        | ((pick_slot == 2) & (column == 1))
        | ((pick_slot == 3) & (column == LANES - 1))
        | ((pick_slot == 4) & (column == 2 * LANES - 1))
    )
    pick = jnp.where(picked, 1.0, 0.0).astype(BF16)
    edge_f32[...] = jnp.zeros_like(edge_f32)
    pred_pad[...] = jnp.zeros_like(pred_pad)
    for layer in range(LAYERS):
        base = layer * 2 * LANES
        edge_f32[layer * SLOTS : (layer + 1) * SLOTS, 0:rows] = rows_dot(
            pick, k_ref[:, base : base + 2 * LANES]
        )
    edge[...] = edge_f32[...].astype(BF16)
    send(edge, edges.at[0], 1, vox_peer(nv - 1))
    send(edge, edges.at[1], 1, vox_peer(1))

    inner = jnp.zeros((8, LANES), F32)
    for layer in range(LAYERS):
        base = layer * 2 * LANES
        at = layer * SLOTS
        smooth = init_ref[:, base : base + LANES]
        detail = init_ref[:, base + LANES : base + 2 * LANES]
        even = smooth - 0.25 * (turn(detail, 1) + detail)
        odd = detail + 0.5 * (even + turn(even, -1))
        inner = jnp.where(lane == at + 1, turn(even, at), inner)
        inner = jnp.where(lane == at + 4, turn(even, at + 5), inner)
        even = jnp.where(lane == 0, 0.0, even)
        odd = jnp.where((lane == 0) | (lane == LANES - 1), 0.0, odd)
        model[:, base : base + LANES] = even.astype(BF16)
        model[:, base + LANES : base + 2 * LANES] = odd.astype(BF16)
    pred_pad[:, 0:rows] = rows_dot(model[...], k_ref[...])
    pred_inner = pred_pad[...]
    detail_first = turn(packed, -1)

    wait(packs, recv_sem, 0)
    after = packs[0]
    before = packs[1]
    even_first = packed - 0.25 * (turn(before, -4) + detail_first)
    odd_first = packed + 0.5 * (turn(even_first, 1) + inner)
    even_after = turn(after, 4) - 0.25 * (packed + turn(after, 3))
    odd_last = packed + 0.5 * (inner + even_after)
    rim = jnp.where(
        slot == 0,
        even_first,
        jnp.where(slot == 1, odd_first, jnp.where(slot == 4, odd_last, 0.0)),
    )
    padded = pred_inner + jnp.dot(rim.astype(BF16), edge[...], preferred_element_type=F32)

    state = []
    for it in range(2):
        phase = 2 + 4 * it
        shared = padded[0:4] + pltpu.roll(padded[4:8], rows, 1)
        pred_send[it] = shared
        preds[it, vox] = shared
        for k in vox_order:
            send(pred_send.at[it], preds.at[it, vox], phase, vox_peer(k))

        if it == 0:
            loads[2].wait()
            loads[3].wait()
            mine = pl.ds(pl.multiple_of(g * width, width), width)
            back = lax.rem(LANES - g * (per * SLOTS), LANES)
            after = pltpu.roll(after, back, 1)
            before = pltpu.roll(before, back, 1)
            pred_pad[:, 64:80] = thr_ref[:, 0, :]
            pred_pad[:, 96:112] = thr_ref[:, 1, :]
            cutoffs = pltpu.roll(pred_pad[...], lax.rem(LANES - g * per, LANES), 1)
            own = init_ref[:, mine]
            cuts = []
            for i in range(per):
                base = i * 2 * LANES
                at = i * SLOTS
                cuts.append(
                    tuple(
                        jnp.broadcast_to(cutoffs[:, c + i : c + i + 1], (8, LANES))
                        for c in (64, 96)
                    )
                )
                state.append(
                    (
                        own[:, base : base + LANES],
                        own[:, base + LANES : base + 2 * LANES],
                        before[:, at + 4 : at + 5],
                        after[:, at : at + 1],
                        after[:, at + 1 : at + 2],
                    )
                )
            wait(edges, recv_sem, 1)
            place = lax.rem(
                lax.broadcasted_iota(jnp.int32, (LAYERS * SLOTS, LANES), 0), SLOTS
            )
            edge_f32[...] = jnp.where(
                place < 3, edges[0].astype(F32), edges[1].astype(F32)
            )
            beyond = edge_f32[:, 0:rows].astype(BF16)

        wait(preds.at[it, pl.ds(0, nv - 1)], recv_sem, phase)
        total = preds[it, 0]
        for j in range(1, nv):
            total = total + preds[it, j]
        predicted = jnp.concatenate(
            [total[:, 0:rows], pltpu.roll(total, LANES - rows, 1)[:, 0:rows]], axis=0
        )
        residual = obs_ref[...] - predicted
        sent = residual.astype(BF16)

        grad = jnp.dot(sent, k_ref[...], preferred_element_type=F32).astype(BF16)
        edge_grad = rows_dot(sent, beyond).astype(BF16)
        for i in range(groups):
            stage[it, i, :, 0:width] = grad[:, i * width : (i + 1) * width]
            stage[it, i, :, width:] = edge_grad

        def send_part(k, carry):
            other = lax.rem(g + k, groups)
            send(stage.at[it, other], parts.at[it, k - 1], phase + 1, group_peer(k))
            return carry

        lax.fori_loop(1, groups, send_part, 0)
        if it == 1:
            resid_ref[...] = residual
        wait(parts.at[it], recv_sem, phase + 1)
        total = stage[it, g].astype(F32)
        for i in range(groups - 1):
            total = total + parts[it, i].astype(F32)
        total = total.astype(BF16)
        sums_send[it] = total
        sums[it, y] = total
        for k in y_order:
            send(sums_send.at[it], sums.at[it, y], phase + 2, y_peer(k))
        wait(sums.at[it, pl.ds(0, ny - 1)], recv_sem, phase + 2)
        total = sums[it, 0].astype(F32)
        for i in range(1, ny):
            total = total + sums[it, i].astype(F32)
        beside = pltpu.roll(total[:, width:], back, 1)

        for i in range(per):
            base = i * 2 * LANES
            at = i * SLOTS
            even = total[:, base : base + LANES]
            odd = total[:, base + LANES : base + 2 * LANES]
            even_after = beside[:, at : at + 1]
            odd_after = beside[:, at + 1 : at + 2]
            even_after2 = beside[:, at + 2 : at + 3]
            even_before = beside[:, at + 3 : at + 4]
            odd_before = beside[:, at + 4 : at + 5]
            detail = odd - 0.5 * (even + take_next(even, even_after))
            detail_before = odd_before - 0.5 * (even_before + even[:, 0:1])
            smooth = even + 0.25 * (take_prev(detail, detail_before) + detail)
            cut_s, cut_d = cuts[i]
            w_s, w_d, w_db, w_sa, w_da = state[i]
            w_s = shrink(w_s + 0.5 * smooth, cut_s)
            w_d = shrink(w_d + 0.5 * detail, cut_d)
            if it == 0:
                detail_after = odd_after - 0.5 * (even_after + even_after2)
                smooth_after = even_after + 0.25 * (detail[:, LANES - 1 :] + detail_after)
                w_db = shrink(w_db + 0.5 * detail_before, cut_d[:, 0:1])
                w_sa = shrink(w_sa + 0.5 * smooth_after, cut_s[:, 0:1])
                w_da = shrink(w_da + 0.5 * detail_after, cut_d[:, 0:1])
                state[i] = (w_s, w_d, w_db, w_sa, w_da)
                w_s, w_d = inverse_wave(w_s, w_d, w_db, w_sa, w_da)
            target = chunks if it == 0 else finals
            target[g, :, base : base + LANES] = w_s.astype(BF16)
            target[g, :, base + LANES : base + 2 * LANES] = w_d.astype(BF16)

        def send_chunk(k, carry):
            send(target.at[g], target.at[g], phase + 3, group_peer(k))
            return carry

        lax.fori_loop(1, groups, send_chunk, 0)
        wait(target.at[pl.ds(0, groups - 1)], recv_sem, phase + 3)
        if it == 0:
            pred = rows_dot(chunks[0], k_ref[:, 0:width])
            for i in range(1, groups):
                pred = pred + rows_dot(chunks[i], k_ref[:, i * width : (i + 1) * width])
            pred_pad[...] = jnp.zeros_like(pred_pad)
            pred_pad[:, 0:rows] = pred
            padded = pred_pad[...]
        else:
            for i in range(groups):
                coef_ref[:, i * width : (i + 1) * width] = finals[i]

    wait(packs, send_sem, 0)
    wait(edges, send_sem, 1)
    for it in range(2):
        phase = 2 + 4 * it
        target = chunks if it == 0 else finals
        wait(preds.at[it, pl.ds(0, nv - 1)], send_sem, phase)
        wait(parts.at[it], send_sem, phase + 1)
        wait(sums.at[it, pl.ds(0, ny - 1)], send_sem, phase + 2)
        wait(target.at[pl.ds(0, groups - 1)], send_sem, phase + 3)


def body(sizes, kernels, observed, initial, threshold):
    nc, ny, nz, nv = sizes
    groups = nc * nz
    width = (LAYERS // groups) * 2 * LANES
    vmem = pl.BlockSpec(memory_space=pltpu.VMEM)
    hbm = pl.BlockSpec(memory_space=pltpu.HBM)
    wide = width + LANES
    cutoffs = jnp.transpose(threshold, (0, 2, 1))
    held = [
        pltpu.with_memory_space_constraint(array, pltpu.HBM)
        for array in (kernels, observed, initial, cutoffs)
    ]
    coefficients, residual = pl.pallas_call(
        functools.partial(kernel, sizes),
        out_shape=(
            jax.ShapeDtypeStruct(initial.shape, BF16),
            jax.ShapeDtypeStruct(observed.shape, F32),
        ),
        in_specs=[hbm] * 4,
        out_specs=(vmem, vmem),
        scratch_shapes=[
            pltpu.VMEM(kernels.shape, BF16),
            pltpu.VMEM(observed.shape, F32),
            pltpu.VMEM(initial.shape, F32),
            pltpu.VMEM(cutoffs.shape, F32),
            pltpu.VMEM((8, LANES), F32),
            pltpu.VMEM((2, 8, LANES), F32),
            pltpu.VMEM((LAYERS * SLOTS, LANES), F32),
            pltpu.VMEM((LAYERS * SLOTS, LANES), BF16),
            pltpu.VMEM((2, LAYERS * SLOTS, LANES), BF16),
            pltpu.VMEM(initial.shape, BF16),
            pltpu.VMEM((8, LANES), F32),
            pltpu.VMEM((2, 4, LANES), F32),
            pltpu.VMEM((2, nv, 4, LANES), F32),
            pltpu.VMEM((2, groups, 8, wide), BF16),
            pltpu.VMEM((2, groups - 1, 8, wide), BF16),
            pltpu.VMEM((2, 8, wide), BF16),
            pltpu.VMEM((2, ny, 8, wide), BF16),
            pltpu.VMEM((groups, 8, width), BF16),
            pltpu.VMEM((groups, 8, width), BF16),
            pltpu.SemaphoreType.DMA((4,)),
            pltpu.SemaphoreType.DMA((10,)),
            pltpu.SemaphoreType.DMA((10,)),
        ],
        compiler_params=pltpu.CompilerParams(
            collective_id=0, has_side_effects=True, vmem_limit_bytes=8 << 20
        ),
    )(*held)
    return coefficients.astype(F32), residual


def build(mesh, sizes):
    return jax.shard_map(
        functools.partial(body, sizes),
        mesh=mesh,
        in_specs=(P("dp", "vox"), P(None, "dp"), P(None, "vox"), P()),
        out_specs=(P(None, "vox"), P(None, "dp")),
        check_vma=False,
    )


def solution(mesh):
    return build(mesh, (NC, NY, NZ, NV))
```

```python
import functools

import jax
import jax.numpy as jnp
from jax import lax
from jax.experimental import pallas as pl
from jax.experimental.pallas import tpu as pltpu
from jax.sharding import PartitionSpec as P

MESH = pl.DeviceIdType.MESH
F32 = jnp.float32
BF16 = jnp.bfloat16
LANES = 128
LAYERS = 16
SLOTS = 8

NC, NY, NZ, NX, NH = 2, 8, 4, 4, 4


def lane_of(rows=8):
    return lax.broadcasted_iota(jnp.int32, (rows, LANES), 1)


def shrink(values, cutoff):
    return jnp.where(
        values > cutoff, values - cutoff, jnp.where(values < -cutoff, values + cutoff, 0.0)
    )


def take_prev(tile, edge):
    return jnp.where(lane_of() == 0, edge, pltpu.roll(tile, 1, 1))


def take_next(tile, edge):
    return jnp.where(lane_of() == LANES - 1, edge, pltpu.roll(tile, LANES - 1, 1))


def inverse_wave(smooth, detail, detail_before, smooth_after, detail_after):
    even = smooth - 0.25 * (take_prev(detail, detail_before) + detail)
    even_after = smooth_after - 0.25 * (detail[:, LANES - 1 :] + detail_after)
    odd = detail + 0.5 * (even + take_next(even, even_after))
    return even, odd


def rows_dot(a, b):
    return lax.dot_general(a, b, (((1,), (1,)), ((), ())), preferred_element_type=F32)


def kernel(
    sizes,
    k_hbm,
    obs_hbm,
    init_hbm,
    thr_hbm,
    coef_ref,
    resid_ref,
    k_ref,
    obs_ref,
    init_ref,
    thr_ref,
    pack,
    packs,
    edge_f32,
    edge,
    edges,
    model,
    pred_pad,
    pred_send,
    preds,
    stage,
    parts,
    sums_send,
    sums,
    chunks,
    finals,
    load_sem,
    send_sem,
    recv_sem,
    beyond_sem,
):
    nc, ny, nz, nx, nh = sizes
    nv = nx * nh
    groups = nc * nz
    per = LAYERS // groups
    width = per * 2 * LANES
    rows = k_ref.shape[0]
    dp = lax.axis_index("dp")
    vox = lax.axis_index("vox")
    core = lax.rem(dp, nc)
    y = lax.rem(lax.div(dp, nc), ny)
    z = lax.div(dp, nc * ny)
    g = z * nc + core

    loads = [
        pltpu.make_async_copy(init_hbm, init_ref, load_sem.at[0]),
        pltpu.make_async_copy(k_hbm, k_ref, load_sem.at[1]),
        pltpu.make_async_copy(obs_hbm, obs_ref, load_sem.at[2]),
        pltpu.make_async_copy(thr_hbm, thr_ref, load_sem.at[3]),
    ]
    for load in loads:
        load.start()

    x = lax.rem(vox, nx)
    high = lax.div(vox, nx)

    def curve_peer(k):
        return dp, lax.rem(vox + k, nv)

    def vox_peer(by):
        dh, dx = by
        return dp, lax.rem(high + dh, nh) * nx + lax.rem(x + dx, nx)

    def group_peer(k):
        other = lax.rem(g + k, groups)
        return (lax.div(other, nc) * ny + y) * nc + lax.rem(other, nc), vox

    def y_peer(k):
        return (z * ny + lax.rem(y + k, ny)) * nc + core, vox

    vox_order = sorted(
        ((dh, dx) for dh in range(nh) for dx in range(nx) if dh or dx),
        key=lambda by: -(nz * min(by[0], nh - by[0]) + min(by[1], nx - by[1])),
    )
    near = [by for by in vox_order if min(by[0], nh - by[0]) < 2]
    y_order = sorted(range(1, ny), key=lambda k: -min(k, ny - k))

    barrier = pltpu.get_barrier_semaphore()

    def greet(peer, k):
        pl.semaphore_signal(barrier, inc=1, device_id=peer(k), device_id_type=MESH)

    for by in near:
        greet(vox_peer, by)
    for k in y_order:
        greet(y_peer, k)
    for k in range(1, groups):
        greet(group_peer, k)

    def send(src, dst, phase, device):
        pltpu.make_async_remote_copy(
            src_ref=src,
            dst_ref=dst,
            send_sem=send_sem.at[phase],
            recv_sem=recv_sem.at[phase],
            device_id=device,
            device_id_type=MESH,
        ).start()

    def wait(ref, sem, phase):
        pltpu.make_async_copy(ref, ref, sem.at[phase]).wait()

    def turn(tile, by):
        by = by % LANES
        return pltpu.roll(tile, by, 1) if by else tile

    lane = lane_of()
    slot = lax.rem(lane, SLOTS)
    loads[0].wait()
    packed = jnp.zeros((8, LANES), F32)
    for layer in range(LAYERS):
        base = layer * 2 * LANES
        smooth = init_ref[:, base : base + LANES]
        detail = init_ref[:, base + LANES : base + 2 * LANES]
        at = layer * SLOTS
        packed = jnp.where(lane == at, turn(smooth, at), packed)
        packed = jnp.where(lane == at + 1, turn(detail, at + 1), packed)
        packed = jnp.where(lane == at + 4, turn(detail, at + 5), packed)
    pack[...] = packed

    pl.semaphore_wait(barrier, len(near) + (groups - 1) + (ny - 1))
    pl.semaphore_signal(
        beyond_sem, inc=1, device_id=vox_peer((nh - 1, 0)), device_id_type=MESH
    )

    send(pack, packs.at[0], 0, curve_peer(nv - 1))
    send(pack, packs.at[1], 0, curve_peer(1))

    loads[1].wait()
    pick_slot = lax.broadcasted_iota(jnp.int32, (SLOTS, 2 * LANES), 0)
    column = lax.broadcasted_iota(jnp.int32, (SLOTS, 2 * LANES), 1)
    picked = (
        ((pick_slot == 0) & (column == 0))
        | ((pick_slot == 1) & (column == LANES))
        | ((pick_slot == 2) & (column == 1))
        | ((pick_slot == 3) & (column == LANES - 1))
        | ((pick_slot == 4) & (column == 2 * LANES - 1))
    )
    pick = jnp.where(picked, 1.0, 0.0).astype(BF16)
    edge_f32[...] = jnp.zeros_like(edge_f32)
    pred_pad[...] = jnp.zeros_like(pred_pad)
    for layer in range(LAYERS):
        base = layer * 2 * LANES
        edge_f32[layer * SLOTS : (layer + 1) * SLOTS, 0:rows] = rows_dot(
            pick, k_ref[:, base : base + 2 * LANES]
        )
    edge[...] = edge_f32[...].astype(BF16)
    send(edge, edges.at[0], 1, curve_peer(nv - 1))
    send(edge, edges.at[1], 1, curve_peer(1))

    inner = jnp.zeros((8, LANES), F32)
    for layer in range(LAYERS):
        base = layer * 2 * LANES
        at = layer * SLOTS
        smooth = init_ref[:, base : base + LANES]
        detail = init_ref[:, base + LANES : base + 2 * LANES]
        even = smooth - 0.25 * (turn(detail, 1) + detail)
        odd = detail + 0.5 * (even + turn(even, -1))
        inner = jnp.where(lane == at + 1, turn(even, at), inner)
        inner = jnp.where(lane == at + 4, turn(even, at + 5), inner)
        even = jnp.where(lane == 0, 0.0, even)
        odd = jnp.where((lane == 0) | (lane == LANES - 1), 0.0, odd)
        model[:, base : base + LANES] = even.astype(BF16)
        model[:, base + LANES : base + 2 * LANES] = odd.astype(BF16)
    pred_pad[:, 0:rows] = rows_dot(model[...], k_ref[...])
    pred_inner = pred_pad[...]
    detail_first = turn(packed, -1)

    wait(packs, recv_sem, 0)
    after = packs[0]
    before = packs[1]
    even_first = packed - 0.25 * (turn(before, -4) + detail_first)
    odd_first = packed + 0.5 * (turn(even_first, 1) + inner)
    even_after = turn(after, 4) - 0.25 * (packed + turn(after, 3))
    odd_last = packed + 0.5 * (inner + even_after)
    rim = jnp.where(
        slot == 0,
        even_first,
        jnp.where(slot == 1, odd_first, jnp.where(slot == 4, odd_last, 0.0)),
    )
    padded = pred_inner + jnp.dot(rim.astype(BF16), edge[...], preferred_element_type=F32)

    state = []
    for it in range(2):
        phase = 2 + 4 * it
        shared = padded[0:4] + pltpu.roll(padded[4:8], rows, 1)
        pred_send[it] = shared
        preds[it, vox] = shared
        if it == 0:
            pl.semaphore_wait(beyond_sem, 1)
        for by in vox_order:
            send(pred_send.at[it], preds.at[it, vox], phase, vox_peer(by))

        if it == 0:
            loads[2].wait()
            loads[3].wait()
            mine = pl.ds(pl.multiple_of(g * width, width), width)
            back = lax.rem(LANES - g * (per * SLOTS), LANES)
            after = pltpu.roll(after, back, 1)
            before = pltpu.roll(before, back, 1)
            pred_pad[:, 64:80] = thr_ref[:, 0, :]
            pred_pad[:, 96:112] = thr_ref[:, 1, :]
            cutoffs = pltpu.roll(pred_pad[...], lax.rem(LANES - g * per, LANES), 1)
            own = init_ref[:, mine]
            cuts = []
            for i in range(per):
                base = i * 2 * LANES
                at = i * SLOTS
                cuts.append(
                    tuple(
                        jnp.broadcast_to(cutoffs[:, c + i : c + i + 1], (8, LANES))
                        for c in (64, 96)
                    )
                )
                state.append(
                    (
                        own[:, base : base + LANES],
                        own[:, base + LANES : base + 2 * LANES],
                        before[:, at + 4 : at + 5],
                        after[:, at : at + 1],
                        after[:, at + 1 : at + 2],
                    )
                )
            wait(edges, recv_sem, 1)
            place = lax.rem(
                lax.broadcasted_iota(jnp.int32, (LAYERS * SLOTS, LANES), 0), SLOTS
            )
            edge_f32[...] = jnp.where(
                place < 3, edges[0].astype(F32), edges[1].astype(F32)
            )
            beyond = edge_f32[:, 0:rows].astype(BF16)

        wait(preds.at[it, pl.ds(0, nv - 1)], recv_sem, phase)
        total = preds[it, 0]
        for j in range(1, nv):
            total = total + preds[it, j]
        predicted = jnp.concatenate(
            [total[:, 0:rows], pltpu.roll(total, LANES - rows, 1)[:, 0:rows]], axis=0
        )
        residual = obs_ref[...] - predicted
        sent = residual.astype(BF16)

        grad = jnp.dot(sent, k_ref[...], preferred_element_type=F32).astype(BF16)
        edge_grad = rows_dot(sent, beyond).astype(BF16)
        for i in range(groups):
            stage[it, i, :, 0:width] = grad[:, i * width : (i + 1) * width]
            stage[it, i, :, width:] = edge_grad

        def send_part(k, carry):
            other = lax.rem(g + k, groups)
            send(stage.at[it, other], parts.at[it, k - 1], phase + 1, group_peer(k))
            return carry

        lax.fori_loop(1, groups, send_part, 0)
        if it == 1:
            resid_ref[...] = residual
        wait(parts.at[it], recv_sem, phase + 1)
        total = stage[it, g].astype(F32)
        for i in range(groups - 1):
            total = total + parts[it, i].astype(F32)
        total = total.astype(BF16)
        sums_send[it] = total
        sums[it, y] = total
        for k in y_order:
            send(sums_send.at[it], sums.at[it, y], phase + 2, y_peer(k))
        wait(sums.at[it, pl.ds(0, ny - 1)], recv_sem, phase + 2)
        total = sums[it, 0].astype(F32)
        for i in range(1, ny):
            total = total + sums[it, i].astype(F32)
        beside = pltpu.roll(total[:, width:], back, 1)

        for i in range(per):
            base = i * 2 * LANES
            at = i * SLOTS
            even = total[:, base : base + LANES]
            odd = total[:, base + LANES : base + 2 * LANES]
            even_after = beside[:, at : at + 1]
            odd_after = beside[:, at + 1 : at + 2]
            even_after2 = beside[:, at + 2 : at + 3]
            even_before = beside[:, at + 3 : at + 4]
            odd_before = beside[:, at + 4 : at + 5]
            detail = odd - 0.5 * (even + take_next(even, even_after))
            detail_before = odd_before - 0.5 * (even_before + even[:, 0:1])
            smooth = even + 0.25 * (take_prev(detail, detail_before) + detail)
            cut_s, cut_d = cuts[i]
            w_s, w_d, w_db, w_sa, w_da = state[i]
            w_s = shrink(w_s + 0.5 * smooth, cut_s)
            w_d = shrink(w_d + 0.5 * detail, cut_d)
            if it == 0:
                detail_after = odd_after - 0.5 * (even_after + even_after2)
                smooth_after = even_after + 0.25 * (detail[:, LANES - 1 :] + detail_after)
                w_db = shrink(w_db + 0.5 * detail_before, cut_d[:, 0:1])
                w_sa = shrink(w_sa + 0.5 * smooth_after, cut_s[:, 0:1])
                w_da = shrink(w_da + 0.5 * detail_after, cut_d[:, 0:1])
                state[i] = (w_s, w_d, w_db, w_sa, w_da)
                w_s, w_d = inverse_wave(w_s, w_d, w_db, w_sa, w_da)
            target = chunks if it == 0 else finals
            target[g, :, base : base + LANES] = w_s.astype(BF16)
            target[g, :, base + LANES : base + 2 * LANES] = w_d.astype(BF16)

        def send_chunk(k, carry):
            send(target.at[g], target.at[g], phase + 3, group_peer(k))
            return carry

        lax.fori_loop(1, groups, send_chunk, 0)
        wait(target.at[pl.ds(0, groups - 1)], recv_sem, phase + 3)
        if it == 0:
            pred = rows_dot(chunks[0], k_ref[:, 0:width])
            for i in range(1, groups):
                pred = pred + rows_dot(chunks[i], k_ref[:, i * width : (i + 1) * width])
            pred_pad[...] = jnp.zeros_like(pred_pad)
            pred_pad[:, 0:rows] = pred
            padded = pred_pad[...]
        else:
            for i in range(groups):
                coef_ref[:, i * width : (i + 1) * width] = finals[i]

    wait(packs, send_sem, 0)
    wait(edges, send_sem, 1)
    for it in range(2):
        phase = 2 + 4 * it
        target = chunks if it == 0 else finals
        wait(preds.at[it, pl.ds(0, nv - 1)], send_sem, phase)
        wait(parts.at[it], send_sem, phase + 1)
        wait(sums.at[it, pl.ds(0, ny - 1)], send_sem, phase + 2)
        wait(target.at[pl.ds(0, groups - 1)], send_sem, phase + 3)


def body(sizes, kernels, observed, initial, threshold):
    nc, ny, nz, nx, nh = sizes
    nv = nx * nh
    groups = nc * nz
    width = (LAYERS // groups) * 2 * LANES
    vmem = pl.BlockSpec(memory_space=pltpu.VMEM)
    hbm = pl.BlockSpec(memory_space=pltpu.HBM)
    wide = width + LANES
    cutoffs = jnp.transpose(threshold, (0, 2, 1))
    held = [
        pltpu.with_memory_space_constraint(array, pltpu.HBM)
        for array in (kernels, observed, initial, cutoffs)
    ]
    coefficients, residual = pl.pallas_call(
        functools.partial(kernel, sizes),
        out_shape=(
            jax.ShapeDtypeStruct(initial.shape, BF16),
            jax.ShapeDtypeStruct(observed.shape, F32),
        ),
        in_specs=[hbm] * 4,
        out_specs=(vmem, vmem),
        scratch_shapes=[
            pltpu.VMEM(kernels.shape, BF16),
            pltpu.VMEM(observed.shape, F32),
            pltpu.VMEM(initial.shape, F32),
            pltpu.VMEM(cutoffs.shape, F32),
            pltpu.VMEM((8, LANES), F32),
            pltpu.VMEM((2, 8, LANES), F32),
            pltpu.VMEM((LAYERS * SLOTS, LANES), F32),
            pltpu.VMEM((LAYERS * SLOTS, LANES), BF16),
            pltpu.VMEM((2, LAYERS * SLOTS, LANES), BF16),
            pltpu.VMEM(initial.shape, BF16),
            pltpu.VMEM((8, LANES), F32),
            pltpu.VMEM((2, 4, LANES), F32),
            pltpu.VMEM((2, nv, 4, LANES), F32),
            pltpu.VMEM((2, groups, 8, wide), BF16),
            pltpu.VMEM((2, groups - 1, 8, wide), BF16),
            pltpu.VMEM((2, 8, wide), BF16),
            pltpu.VMEM((2, ny, 8, wide), BF16),
            pltpu.VMEM((groups, 8, width), BF16),
            pltpu.VMEM((groups, 8, width), BF16),
            pltpu.SemaphoreType.DMA((4,)),
            pltpu.SemaphoreType.DMA((10,)),
            pltpu.SemaphoreType.DMA((10,)),
            pltpu.SemaphoreType.REGULAR,
        ],
        compiler_params=pltpu.CompilerParams(
            collective_id=0, has_side_effects=True, vmem_limit_bytes=8 << 20
        ),
    )(*held)
    return coefficients.astype(F32), residual


def build(mesh, sizes):
    return jax.shard_map(
        functools.partial(body, sizes),
        mesh=mesh,
        in_specs=(P("dp", "vox"), P(None, "dp"), P(None, "vox"), P()),
        out_specs=(P(None, "vox"), P(None, "dp")),
        check_vma=False,
    )


def solution(mesh):
    return build(mesh, (NC, NY, NZ, NX, NH))
```

```python
import functools

import jax
import jax.numpy as jnp
from jax import lax
from jax.experimental import pallas as pl
from jax.experimental.pallas import tpu as pltpu
from jax.sharding import PartitionSpec as P

MESH = pl.DeviceIdType.MESH
F32 = jnp.float32
BF16 = jnp.bfloat16
LANES = 128
LAYERS = 16
SLOTS = 8

NC, NY, NZ, NX, NH = 2, 8, 4, 4, 4


def lane_of(rows=8):
    return lax.broadcasted_iota(jnp.int32, (rows, LANES), 1)


def shrink(values, cutoff):
    return jnp.where(
        values > cutoff, values - cutoff, jnp.where(values < -cutoff, values + cutoff, 0.0)
    )


def take_prev(tile, edge):
    return jnp.where(lane_of() == 0, edge, pltpu.roll(tile, 1, 1))


def take_next(tile, edge):
    return jnp.where(lane_of() == LANES - 1, edge, pltpu.roll(tile, LANES - 1, 1))


def inverse_wave(smooth, detail, detail_before, smooth_after, detail_after):
    even = smooth - 0.25 * (take_prev(detail, detail_before) + detail)
    even_after = smooth_after - 0.25 * (detail[:, LANES - 1 :] + detail_after)
    odd = detail + 0.5 * (even + take_next(even, even_after))
    return even, odd


def rows_dot(a, b):
    return lax.dot_general(a, b, (((1,), (1,)), ((), ())), preferred_element_type=F32)


def kernel(
    sizes,
    k_hbm,
    obs_hbm,
    init_hbm,
    thr_hbm,
    coef_ref,
    resid_ref,
    k_ref,
    obs_ref,
    init_ref,
    thr_ref,
    pack,
    packs,
    edge_f32,
    edge,
    edges,
    model,
    pred_pad,
    pred_send,
    preds,
    stage,
    parts,
    sums_send,
    sums,
    chunks,
    finals,
    load_sem,
    send_sem,
    recv_sem,
    beyond_sem,
):
    nc, ny, nz, nx, nh = sizes
    nv = nx * nh
    groups = nc * nz
    per = LAYERS // groups
    width = per * 2 * LANES
    rows = k_ref.shape[0]
    dp = lax.axis_index("dp")
    vox = lax.axis_index("vox")
    core = lax.rem(dp, nc)
    y = lax.rem(lax.div(dp, nc), ny)
    z = lax.div(dp, nc * ny)
    g = z * nc + core

    loads = [
        pltpu.make_async_copy(init_hbm, init_ref, load_sem.at[0]),
        pltpu.make_async_copy(k_hbm, k_ref, load_sem.at[1]),
        pltpu.make_async_copy(obs_hbm, obs_ref, load_sem.at[2]),
        pltpu.make_async_copy(thr_hbm, thr_ref, load_sem.at[3]),
    ]
    for load in loads:
        load.start()

    x = lax.rem(vox, nx)
    high = lax.div(vox, nx)

    def curve_peer(k):
        return dp, lax.rem(vox + k, nv)

    def vox_peer(by):
        dh, dx = by
        return dp, lax.rem(high + dh, nh) * nx + lax.rem(x + dx, nx)

    group_order = []
    if nz == 4:
        group_order += [(nz - 1 - z, c) for c in range(nc)]
        group_order += [(lax.rem(z + 2, nz), c) for c in range(nc)]
    group_order += [(z + 1 - 2 * lax.rem(z, 2), c) for c in range(nc)]
    group_order += [(z, c) for c in range(1, nc)]
    group_order = [(oz, lax.rem(core + c, nc)) for oz, c in group_order]
    group_order = [(oz * nc + oc, (oz * ny + y) * nc + oc) for oz, oc in group_order]

    def y_peer(k):
        return (z * ny + lax.rem(y + k, ny)) * nc + core, vox

    vox_order = sorted(
        ((dh, dx) for dh in range(nh) for dx in range(nx) if dh or dx),
        key=lambda by: -(nz * min(by[0], nh - by[0]) + min(by[1], nx - by[1])),
    )
    near = [by for by in vox_order if min(by[0], nh - by[0]) < 2]
    y_order = sorted(range(1, ny), key=lambda k: -min(k, ny - k))

    barrier = pltpu.get_barrier_semaphore()

    def greet(peer, k):
        pl.semaphore_signal(barrier, inc=1, device_id=peer(k), device_id_type=MESH)

    for by in near:
        greet(vox_peer, by)
    for k in y_order:
        greet(y_peer, k)
    for _, other in group_order:
        pl.semaphore_signal(
            barrier, inc=1, device_id=(other, vox), device_id_type=MESH
        )

    def send(src, dst, phase, device):
        pltpu.make_async_remote_copy(
            src_ref=src,
            dst_ref=dst,
            send_sem=send_sem.at[phase],
            recv_sem=recv_sem.at[phase],
            device_id=device,
            device_id_type=MESH,
        ).start()

    def wait(ref, sem, phase):
        pltpu.make_async_copy(ref, ref, sem.at[phase]).wait()

    def turn(tile, by):
        by = by % LANES
        return pltpu.roll(tile, by, 1) if by else tile

    lane = lane_of()
    slot = lax.rem(lane, SLOTS)
    loads[0].wait()
    packed = jnp.zeros((8, LANES), F32)
    for layer in range(LAYERS):
        base = layer * 2 * LANES
        smooth = init_ref[:, base : base + LANES]
        detail = init_ref[:, base + LANES : base + 2 * LANES]
        at = layer * SLOTS
        packed = jnp.where(lane == at, turn(smooth, at), packed)
        packed = jnp.where(lane == at + 1, turn(detail, at + 1), packed)
        packed = jnp.where(lane == at + 4, turn(detail, at + 5), packed)
    pack[...] = packed

    pl.semaphore_wait(barrier, len(near) + (groups - 1) + (ny - 1))
    pl.semaphore_signal(
        beyond_sem, inc=1, device_id=vox_peer((nh - 1, 0)), device_id_type=MESH
    )

    send(pack, packs.at[0], 0, curve_peer(nv - 1))
    send(pack, packs.at[1], 0, curve_peer(1))

    loads[1].wait()
    pick_slot = lax.broadcasted_iota(jnp.int32, (SLOTS, 2 * LANES), 0)
    column = lax.broadcasted_iota(jnp.int32, (SLOTS, 2 * LANES), 1)
    picked = (
        ((pick_slot == 0) & (column == 0))
        | ((pick_slot == 1) & (column == LANES))
        | ((pick_slot == 2) & (column == 1))
        | ((pick_slot == 3) & (column == LANES - 1))
        | ((pick_slot == 4) & (column == 2 * LANES - 1))
    )
    pick = jnp.where(picked, 1.0, 0.0).astype(BF16)
    edge_f32[...] = jnp.zeros_like(edge_f32)
    pred_pad[...] = jnp.zeros_like(pred_pad)
    for layer in range(LAYERS):
        base = layer * 2 * LANES
        edge_f32[layer * SLOTS : (layer + 1) * SLOTS, 0:rows] = rows_dot(
            pick, k_ref[:, base : base + 2 * LANES]
        )
    edge[...] = edge_f32[...].astype(BF16)
    send(edge, edges.at[0], 1, curve_peer(nv - 1))
    send(edge, edges.at[1], 1, curve_peer(1))

    inner = jnp.zeros((8, LANES), F32)
    for layer in range(LAYERS):
        base = layer * 2 * LANES
        at = layer * SLOTS
        smooth = init_ref[:, base : base + LANES]
        detail = init_ref[:, base + LANES : base + 2 * LANES]
        even = smooth - 0.25 * (turn(detail, 1) + detail)
        odd = detail + 0.5 * (even + turn(even, -1))
        inner = jnp.where(lane == at + 1, turn(even, at), inner)
        inner = jnp.where(lane == at + 4, turn(even, at + 5), inner)
        even = jnp.where(lane == 0, 0.0, even)
        odd = jnp.where((lane == 0) | (lane == LANES - 1), 0.0, odd)
        model[:, base : base + LANES] = even.astype(BF16)
        model[:, base + LANES : base + 2 * LANES] = odd.astype(BF16)
    pred_pad[:, 0:rows] = rows_dot(model[...], k_ref[...])
    pred_inner = pred_pad[...]
    detail_first = turn(packed, -1)

    wait(packs, recv_sem, 0)
    after = packs[0]
    before = packs[1]
    even_first = packed - 0.25 * (turn(before, -4) + detail_first)
    odd_first = packed + 0.5 * (turn(even_first, 1) + inner)
    even_after = turn(after, 4) - 0.25 * (packed + turn(after, 3))
    odd_last = packed + 0.5 * (inner + even_after)
    rim = jnp.where(
        slot == 0,
        even_first,
        jnp.where(slot == 1, odd_first, jnp.where(slot == 4, odd_last, 0.0)),
    )
    padded = pred_inner + jnp.dot(rim.astype(BF16), edge[...], preferred_element_type=F32)

    state = []
    for it in range(2):
        phase = 2 + 4 * it
        shared = padded[0:4] + pltpu.roll(padded[4:8], rows, 1)
        pred_send[it] = shared
        preds[it, vox] = shared
        if it == 0:
            pl.semaphore_wait(beyond_sem, 1)
        for by in vox_order:
            send(pred_send.at[it], preds.at[it, vox], phase, vox_peer(by))

        if it == 0:
            loads[2].wait()
            loads[3].wait()
            mine = pl.ds(pl.multiple_of(g * width, width), width)
            back = lax.rem(LANES - g * (per * SLOTS), LANES)
            after = pltpu.roll(after, back, 1)
            before = pltpu.roll(before, back, 1)
            pred_pad[:, 64:80] = thr_ref[:, 0, :]
            pred_pad[:, 96:112] = thr_ref[:, 1, :]
            cutoffs = pltpu.roll(pred_pad[...], lax.rem(LANES - g * per, LANES), 1)
            own = init_ref[:, mine]
            cuts = []
            for i in range(per):
                base = i * 2 * LANES
                at = i * SLOTS
                cuts.append(
                    tuple(
                        jnp.broadcast_to(cutoffs[:, c + i : c + i + 1], (8, LANES))
                        for c in (64, 96)
                    )
                )
                state.append(
                    (
                        own[:, base : base + LANES],
                        own[:, base + LANES : base + 2 * LANES],
                        before[:, at + 4 : at + 5],
                        after[:, at : at + 1],
                        after[:, at + 1 : at + 2],
                    )
                )
            wait(edges, recv_sem, 1)
            place = lax.rem(
                lax.broadcasted_iota(jnp.int32, (LAYERS * SLOTS, LANES), 0), SLOTS
            )
            edge_f32[...] = jnp.where(
                place < 3, edges[0].astype(F32), edges[1].astype(F32)
            )
            beyond = edge_f32[:, 0:rows].astype(BF16)

        wait(preds.at[it, pl.ds(0, nv - 1)], recv_sem, phase)
        total = preds[it, 0]
        for j in range(1, nv):
            total = total + preds[it, j]
        predicted = jnp.concatenate(
            [total[:, 0:rows], pltpu.roll(total, LANES - rows, 1)[:, 0:rows]], axis=0
        )
        residual = obs_ref[...] - predicted
        sent = residual.astype(BF16)

        grad = jnp.dot(sent, k_ref[...], preferred_element_type=F32).astype(BF16)
        edge_grad = rows_dot(sent, beyond).astype(BF16)
        for i in range(groups):
            stage[it, i, :, 0:width] = grad[:, i * width : (i + 1) * width]
            stage[it, i, :, width:] = edge_grad

        for i, (chunk, other) in enumerate(group_order):
            send(stage.at[it, chunk], parts.at[it, i], phase + 1, (other, vox))
        if it == 1:
            resid_ref[...] = residual
        wait(parts.at[it], recv_sem, phase + 1)
        total = stage[it, g].astype(F32)
        for i in range(groups - 1):
            total = total + parts[it, i].astype(F32)
        total = total.astype(BF16)
        sums_send[it] = total
        sums[it, y] = total
        for k in y_order:
            send(sums_send.at[it], sums.at[it, y], phase + 2, y_peer(k))
        wait(sums.at[it, pl.ds(0, ny - 1)], recv_sem, phase + 2)
        total = sums[it, 0].astype(F32)
        for i in range(1, ny):
            total = total + sums[it, i].astype(F32)
        beside = pltpu.roll(total[:, width:], back, 1)

        for i in range(per):
            base = i * 2 * LANES
            at = i * SLOTS
            even = total[:, base : base + LANES]
            odd = total[:, base + LANES : base + 2 * LANES]
            even_after = beside[:, at : at + 1]
            odd_after = beside[:, at + 1 : at + 2]
            even_after2 = beside[:, at + 2 : at + 3]
            even_before = beside[:, at + 3 : at + 4]
            odd_before = beside[:, at + 4 : at + 5]
            detail = odd - 0.5 * (even + take_next(even, even_after))
            detail_before = odd_before - 0.5 * (even_before + even[:, 0:1])
            smooth = even + 0.25 * (take_prev(detail, detail_before) + detail)
            cut_s, cut_d = cuts[i]
            w_s, w_d, w_db, w_sa, w_da = state[i]
            w_s = shrink(w_s + 0.5 * smooth, cut_s)
            w_d = shrink(w_d + 0.5 * detail, cut_d)
            if it == 0:
                detail_after = odd_after - 0.5 * (even_after + even_after2)
                smooth_after = even_after + 0.25 * (detail[:, LANES - 1 :] + detail_after)
                w_db = shrink(w_db + 0.5 * detail_before, cut_d[:, 0:1])
                w_sa = shrink(w_sa + 0.5 * smooth_after, cut_s[:, 0:1])
                w_da = shrink(w_da + 0.5 * detail_after, cut_d[:, 0:1])
                state[i] = (w_s, w_d, w_db, w_sa, w_da)
                w_s, w_d = inverse_wave(w_s, w_d, w_db, w_sa, w_da)
            target = chunks if it == 0 else finals
            target[g, :, base : base + LANES] = w_s.astype(BF16)
            target[g, :, base + LANES : base + 2 * LANES] = w_d.astype(BF16)

        for _, other in group_order:
            send(target.at[g], target.at[g], phase + 3, (other, vox))
        wait(target.at[pl.ds(0, groups - 1)], recv_sem, phase + 3)
        if it == 0:
            pred = rows_dot(chunks[0], k_ref[:, 0:width])
            for i in range(1, groups):
                pred = pred + rows_dot(chunks[i], k_ref[:, i * width : (i + 1) * width])
            pred_pad[...] = jnp.zeros_like(pred_pad)
            pred_pad[:, 0:rows] = pred
            padded = pred_pad[...]
        else:
            for i in range(groups):
                coef_ref[:, i * width : (i + 1) * width] = finals[i]

    wait(packs, send_sem, 0)
    wait(edges, send_sem, 1)
    for it in range(2):
        phase = 2 + 4 * it
        target = chunks if it == 0 else finals
        wait(preds.at[it, pl.ds(0, nv - 1)], send_sem, phase)
        wait(parts.at[it], send_sem, phase + 1)
        wait(sums.at[it, pl.ds(0, ny - 1)], send_sem, phase + 2)
        wait(target.at[pl.ds(0, groups - 1)], send_sem, phase + 3)


def finish(narrow_ref, held_ref, coef_ref, resid_ref):
    coef_ref[...] = narrow_ref[...].astype(F32)
    resid_ref[...] = held_ref[...]


def body(sizes, kernels, observed, initial, threshold):
    nc, ny, nz, nx, nh = sizes
    nv = nx * nh
    groups = nc * nz
    width = (LAYERS // groups) * 2 * LANES
    vmem = pl.BlockSpec(memory_space=pltpu.VMEM)
    hbm = pl.BlockSpec(memory_space=pltpu.HBM)
    wide = width + LANES
    cutoffs = jnp.transpose(threshold, (0, 2, 1))
    held = [
        pltpu.with_memory_space_constraint(array, pltpu.HBM)
        for array in (kernels, observed, initial, cutoffs)
    ]
    coefficients, residual = pl.pallas_call(
        functools.partial(kernel, sizes),
        out_shape=(
            jax.ShapeDtypeStruct(initial.shape, BF16),
            jax.ShapeDtypeStruct(observed.shape, F32),
        ),
        in_specs=[hbm] * 4,
        out_specs=(vmem, vmem),
        scratch_shapes=[
            pltpu.VMEM(kernels.shape, BF16),
            pltpu.VMEM(observed.shape, F32),
            pltpu.VMEM(initial.shape, F32),
            pltpu.VMEM(cutoffs.shape, F32),
            pltpu.VMEM((8, LANES), F32),
            pltpu.VMEM((2, 8, LANES), F32),
            pltpu.VMEM((LAYERS * SLOTS, LANES), F32),
            pltpu.VMEM((LAYERS * SLOTS, LANES), BF16),
            pltpu.VMEM((2, LAYERS * SLOTS, LANES), BF16),
            pltpu.VMEM(initial.shape, BF16),
            pltpu.VMEM((8, LANES), F32),
            pltpu.VMEM((2, 4, LANES), F32),
            pltpu.VMEM((2, nv, 4, LANES), F32),
            pltpu.VMEM((2, groups, 8, wide), BF16),
            pltpu.VMEM((2, groups - 1, 8, wide), BF16),
            pltpu.VMEM((2, 8, wide), BF16),
            pltpu.VMEM((2, ny, 8, wide), BF16),
            pltpu.VMEM((groups, 8, width), BF16),
            pltpu.VMEM((groups, 8, width), BF16),
            pltpu.SemaphoreType.DMA((4,)),
            pltpu.SemaphoreType.DMA((10,)),
            pltpu.SemaphoreType.DMA((10,)),
            pltpu.SemaphoreType.REGULAR,
        ],
        compiler_params=pltpu.CompilerParams(
            collective_id=0, has_side_effects=True, vmem_limit_bytes=8 << 20
        ),
    )(*held)
    return pl.pallas_call(
        finish,
        out_shape=(
            jax.ShapeDtypeStruct(initial.shape, F32),
            jax.ShapeDtypeStruct(observed.shape, F32),
        ),
        in_specs=[vmem] * 2,
        out_specs=(vmem, vmem),
        compiler_params=pltpu.CompilerParams(vmem_limit_bytes=8 << 20),
    )(coefficients, residual)


def build(mesh, sizes):
    return jax.shard_map(
        functools.partial(body, sizes),
        mesh=mesh,
        in_specs=(P("dp", "vox"), P(None, "dp"), P(None, "vox"), P()),
        out_specs=(P(None, "vox"), P(None, "dp")),
        check_vma=False,
    )


def solution(mesh):
    return build(mesh, (NC, NY, NZ, NX, NH))
```

```python
import functools

import jax
import jax.numpy as jnp
from jax import lax
from jax.experimental import pallas as pl
from jax.experimental.pallas import tpu as pltpu
from jax.sharding import PartitionSpec as P

MESH = pl.DeviceIdType.MESH
F32 = jnp.float32
BF16 = jnp.bfloat16
LANES = 128
LAYERS = 16
SLOTS = 8

NC, NY, NZ, NX, NH = 2, 8, 4, 4, 4


def lane_of(rows=8):
    return lax.broadcasted_iota(jnp.int32, (rows, LANES), 1)


def shrink(values, cutoff):
    return jnp.where(
        values > cutoff, values - cutoff, jnp.where(values < -cutoff, values + cutoff, 0.0)
    )


def take_prev(tile, edge):
    return jnp.where(lane_of() == 0, edge, pltpu.roll(tile, 1, 1))


def take_next(tile, edge):
    return jnp.where(lane_of() == LANES - 1, edge, pltpu.roll(tile, LANES - 1, 1))


def inverse_wave(smooth, detail, detail_before, smooth_after, detail_after):
    even = smooth - 0.25 * (take_prev(detail, detail_before) + detail)
    even_after = smooth_after - 0.25 * (detail[:, LANES - 1 :] + detail_after)
    odd = detail + 0.5 * (even + take_next(even, even_after))
    return even, odd


def rows_dot(a, b):
    return lax.dot_general(a, b, (((1,), (1,)), ((), ())), preferred_element_type=F32)


def kernel(
    sizes,
    k_hbm,
    obs_hbm,
    init_hbm,
    thr_hbm,
    coef_ref,
    resid_ref,
    k_ref,
    obs_ref,
    init_ref,
    thr_ref,
    pack,
    packs,
    edge_f32,
    edge,
    edges,
    model,
    pred_pad,
    pred_send,
    preds,
    stage,
    parts,
    sums_send,
    sums,
    chunks,
    finals,
    load_sem,
    send_sem,
    recv_sem,
    beyond_sem,
):
    nc, ny, nz, nx, nh = sizes
    nv = nx * nh
    groups = nc * nz
    per = LAYERS // groups
    width = per * 2 * LANES
    rows = k_ref.shape[0]
    dp = lax.axis_index("dp")
    vox = lax.axis_index("vox")
    core = lax.rem(dp, nc)
    y = lax.rem(lax.div(dp, nc), ny)
    z = lax.div(dp, nc * ny)
    g = z * nc + core

    loads = [
        pltpu.make_async_copy(init_hbm, init_ref, load_sem.at[0]),
        pltpu.make_async_copy(k_hbm, k_ref, load_sem.at[1]),
        pltpu.make_async_copy(obs_hbm, obs_ref, load_sem.at[2]),
        pltpu.make_async_copy(thr_hbm, thr_ref, load_sem.at[3]),
    ]
    for load in loads:
        load.start()

    x = lax.rem(vox, nx)
    high = lax.div(vox, nx)

    def curve_peer(k):
        return dp, lax.rem(vox + k, nv)

    def vox_peer(by):
        dh, dx = by
        return dp, lax.rem(high + dh, nh) * nx + lax.rem(x + dx, nx)

    group_order = []
    if nz == 4:
        group_order += [(nz - 1 - z, c) for c in range(nc)]
        group_order += [(lax.rem(z + 2, nz), c) for c in range(nc)]
    group_order += [(z + 1 - 2 * lax.rem(z, 2), c) for c in range(nc)]
    group_order += [(z, c) for c in range(1, nc)]
    group_order = [(oz, lax.rem(core + c, nc)) for oz, c in group_order]
    group_order = [(oz * nc + oc, (oz * ny + y) * nc + oc) for oz, oc in group_order]

    def y_peer(k):
        return (z * ny + lax.rem(y + k, ny)) * nc + core, vox

    vox_order = sorted(
        ((dh, dx) for dh in range(nh) for dx in range(nx) if dh or dx),
        key=lambda by: -(nz * min(by[0], nh - by[0]) + min(by[1], nx - by[1])),
    )
    near = [by for by in vox_order if min(by[0], nh - by[0]) < 2]
    y_order = sorted(range(1, ny), key=lambda k: -min(k, ny - k))

    barrier = pltpu.get_barrier_semaphore()

    def greet(peer, k):
        pl.semaphore_signal(barrier, inc=1, device_id=peer(k), device_id_type=MESH)

    for k in y_order:
        greet(y_peer, k)
    for by in near:
        greet(vox_peer, by)
    for _, other in group_order:
        pl.semaphore_signal(
            barrier, inc=1, device_id=(other, vox), device_id_type=MESH
        )

    def send(src, dst, phase, device):
        pltpu.make_async_remote_copy(
            src_ref=src,
            dst_ref=dst,
            send_sem=send_sem.at[phase],
            recv_sem=recv_sem.at[phase],
            device_id=device,
            device_id_type=MESH,
        ).start()

    def wait(ref, sem, phase):
        pltpu.make_async_copy(ref, ref, sem.at[phase]).wait()

    def turn(tile, by):
        by = by % LANES
        return pltpu.roll(tile, by, 1) if by else tile

    lane = lane_of()
    slot = lax.rem(lane, SLOTS)
    loads[0].wait()
    packed = jnp.zeros((8, LANES), F32)
    for layer in range(LAYERS):
        base = layer * 2 * LANES
        smooth = init_ref[:, base : base + LANES]
        detail = init_ref[:, base + LANES : base + 2 * LANES]
        at = layer * SLOTS
        packed = jnp.where(lane == at, turn(smooth, at), packed)
        packed = jnp.where(lane == at + 1, turn(detail, at + 1), packed)
        packed = jnp.where(lane == at + 4, turn(detail, at + 5), packed)
    pack[...] = packed

    pl.semaphore_wait(barrier, len(near) + (groups - 1) + (ny - 1))
    pl.semaphore_signal(
        beyond_sem, inc=1, device_id=vox_peer((nh - 1, 0)), device_id_type=MESH
    )

    send(pack, packs.at[0], 0, curve_peer(nv - 1))
    send(pack, packs.at[1], 0, curve_peer(1))

    loads[1].wait()
    pick_slot = lax.broadcasted_iota(jnp.int32, (SLOTS, 2 * LANES), 0)
    column = lax.broadcasted_iota(jnp.int32, (SLOTS, 2 * LANES), 1)
    picked = (
        ((pick_slot == 0) & (column == 0))
        | ((pick_slot == 1) & (column == LANES))
        | ((pick_slot == 2) & (column == 1))
        | ((pick_slot == 3) & (column == LANES - 1))
        | ((pick_slot == 4) & (column == 2 * LANES - 1))
    )
    pick = jnp.where(picked, 1.0, 0.0).astype(BF16)
    edge_f32[...] = jnp.zeros_like(edge_f32)
    pred_pad[...] = jnp.zeros_like(pred_pad)
    for layer in range(LAYERS):
        base = layer * 2 * LANES
        edge_f32[layer * SLOTS : (layer + 1) * SLOTS, 0:rows] = rows_dot(
            pick, k_ref[:, base : base + 2 * LANES]
        )
    edge[...] = edge_f32[...].astype(BF16)

    inner = jnp.zeros((8, LANES), F32)
    for layer in range(LAYERS):
        base = layer * 2 * LANES
        at = layer * SLOTS
        smooth = init_ref[:, base : base + LANES]
        detail = init_ref[:, base + LANES : base + 2 * LANES]
        even = smooth - 0.25 * (turn(detail, 1) + detail)
        odd = detail + 0.5 * (even + turn(even, -1))
        inner = jnp.where(lane == at + 1, turn(even, at), inner)
        inner = jnp.where(lane == at + 4, turn(even, at + 5), inner)
        even = jnp.where(lane == 0, 0.0, even)
        odd = jnp.where((lane == 0) | (lane == LANES - 1), 0.0, odd)
        model[:, base : base + LANES] = even.astype(BF16)
        model[:, base + LANES : base + 2 * LANES] = odd.astype(BF16)
    pred_pad[:, 0:rows] = rows_dot(model[...], k_ref[...])
    pred_inner = pred_pad[...]
    detail_first = turn(packed, -1)

    wait(packs, recv_sem, 0)
    after = packs[0]
    before = packs[1]
    even_first = packed - 0.25 * (turn(before, -4) + detail_first)
    odd_first = packed + 0.5 * (turn(even_first, 1) + inner)
    even_after = turn(after, 4) - 0.25 * (packed + turn(after, 3))
    odd_last = packed + 0.5 * (inner + even_after)
    rim = jnp.where(
        slot == 0,
        even_first,
        jnp.where(slot == 1, odd_first, jnp.where(slot == 4, odd_last, 0.0)),
    )
    padded = pred_inner + jnp.dot(rim.astype(BF16), edge[...], preferred_element_type=F32)

    state = []
    for it in range(2):
        phase = 2 + 4 * it
        shared = padded[0:4] + pltpu.roll(padded[4:8], rows, 1)
        pred_send[it] = shared
        preds[it, vox] = shared
        if it == 0:
            pl.semaphore_wait(beyond_sem, 1)
        for by in vox_order:
            send(pred_send.at[it], preds.at[it, vox], phase, vox_peer(by))

        if it == 0:
            send(edge, edges.at[0], 1, curve_peer(nv - 1))
            send(edge, edges.at[1], 1, curve_peer(1))
            loads[2].wait()
            loads[3].wait()
            mine = pl.ds(pl.multiple_of(g * width, width), width)
            back = lax.rem(LANES - g * (per * SLOTS), LANES)
            after = pltpu.roll(after, back, 1)
            before = pltpu.roll(before, back, 1)
            pred_pad[:, 64:80] = thr_ref[:, 0, :]
            pred_pad[:, 96:112] = thr_ref[:, 1, :]
            cutoffs = pltpu.roll(pred_pad[...], lax.rem(LANES - g * per, LANES), 1)
            own = init_ref[:, mine]
            cuts = []
            for i in range(per):
                base = i * 2 * LANES
                at = i * SLOTS
                cuts.append(
                    tuple(
                        jnp.broadcast_to(cutoffs[:, c + i : c + i + 1], (8, LANES))
                        for c in (64, 96)
                    )
                )
                state.append(
                    (
                        own[:, base : base + LANES],
                        own[:, base + LANES : base + 2 * LANES],
                        before[:, at + 4 : at + 5],
                        after[:, at : at + 1],
                        after[:, at + 1 : at + 2],
                    )
                )
            wait(edges, recv_sem, 1)
            place = lax.rem(
                lax.broadcasted_iota(jnp.int32, (LAYERS * SLOTS, LANES), 0), SLOTS
            )
            edge_f32[...] = jnp.where(
                place < 3, edges[0].astype(F32), edges[1].astype(F32)
            )
            beyond = edge_f32[:, 0:rows].astype(BF16)

        wait(preds.at[it, pl.ds(0, nv - 1)], recv_sem, phase)
        total = preds[it, 0]
        for j in range(1, nv):
            total = total + preds[it, j]
        predicted = jnp.concatenate(
            [total[:, 0:rows], pltpu.roll(total, LANES - rows, 1)[:, 0:rows]], axis=0
        )
        residual = obs_ref[...] - predicted
        sent = residual.astype(BF16)

        grad = jnp.dot(sent, k_ref[...], preferred_element_type=F32).astype(BF16)
        edge_grad = rows_dot(sent, beyond).astype(BF16)
        for i in range(groups):
            stage[it, i, :, 0:width] = grad[:, i * width : (i + 1) * width]
            stage[it, i, :, width:] = edge_grad

        for i, (chunk, other) in enumerate(group_order):
            send(stage.at[it, chunk], parts.at[it, i], phase + 1, (other, vox))
        if it == 1:
            resid_ref[...] = residual
        wait(parts.at[it], recv_sem, phase + 1)
        total = stage[it, g].astype(F32)
        for i in range(groups - 1):
            total = total + parts[it, i].astype(F32)
        total = total.astype(BF16)
        sums_send[it] = total
        sums[it, y] = total
        for k in y_order:
            send(sums_send.at[it], sums.at[it, y], phase + 2, y_peer(k))
        wait(sums.at[it, pl.ds(0, ny - 1)], recv_sem, phase + 2)
        total = sums[it, 0].astype(F32)
        for i in range(1, ny):
            total = total + sums[it, i].astype(F32)
        beside = pltpu.roll(total[:, width:], back, 1)

        for i in range(per):
            base = i * 2 * LANES
            at = i * SLOTS
            even = total[:, base : base + LANES]
            odd = total[:, base + LANES : base + 2 * LANES]
            even_after = beside[:, at : at + 1]
            odd_after = beside[:, at + 1 : at + 2]
            even_after2 = beside[:, at + 2 : at + 3]
            even_before = beside[:, at + 3 : at + 4]
            odd_before = beside[:, at + 4 : at + 5]
            detail = odd - 0.5 * (even + take_next(even, even_after))
            detail_before = odd_before - 0.5 * (even_before + even[:, 0:1])
            smooth = even + 0.25 * (take_prev(detail, detail_before) + detail)
            cut_s, cut_d = cuts[i]
            w_s, w_d, w_db, w_sa, w_da = state[i]
            w_s = shrink(w_s + 0.5 * smooth, cut_s)
            w_d = shrink(w_d + 0.5 * detail, cut_d)
            if it == 0:
                detail_after = odd_after - 0.5 * (even_after + even_after2)
                smooth_after = even_after + 0.25 * (detail[:, LANES - 1 :] + detail_after)
                w_db = shrink(w_db + 0.5 * detail_before, cut_d[:, 0:1])
                w_sa = shrink(w_sa + 0.5 * smooth_after, cut_s[:, 0:1])
                w_da = shrink(w_da + 0.5 * detail_after, cut_d[:, 0:1])
                state[i] = (w_s, w_d, w_db, w_sa, w_da)
                w_s, w_d = inverse_wave(w_s, w_d, w_db, w_sa, w_da)
            target = chunks if it == 0 else finals
            target[g, :, base : base + LANES] = w_s.astype(BF16)
            target[g, :, base + LANES : base + 2 * LANES] = w_d.astype(BF16)

        for _, other in group_order:
            send(target.at[g], target.at[g], phase + 3, (other, vox))
        wait(target.at[pl.ds(0, groups - 1)], recv_sem, phase + 3)
        if it == 0:
            pred = rows_dot(chunks[0], k_ref[:, 0:width])
            for i in range(1, groups):
                pred = pred + rows_dot(chunks[i], k_ref[:, i * width : (i + 1) * width])
            pred_pad[...] = jnp.zeros_like(pred_pad)
            pred_pad[:, 0:rows] = pred
            padded = pred_pad[...]
        else:
            for i in range(groups):
                coef_ref[:, i * width : (i + 1) * width] = finals[i]

    wait(packs, send_sem, 0)
    wait(edges, send_sem, 1)
    for it in range(2):
        phase = 2 + 4 * it
        target = chunks if it == 0 else finals
        wait(preds.at[it, pl.ds(0, nv - 1)], send_sem, phase)
        wait(parts.at[it], send_sem, phase + 1)
        wait(sums.at[it, pl.ds(0, ny - 1)], send_sem, phase + 2)
        wait(target.at[pl.ds(0, groups - 1)], send_sem, phase + 3)


def finish(narrow_ref, held_ref, coef_ref, resid_ref):
    coef_ref[...] = narrow_ref[...].astype(F32)
    resid_ref[...] = held_ref[...]


def body(sizes, kernels, observed, initial, threshold):
    nc, ny, nz, nx, nh = sizes
    nv = nx * nh
    groups = nc * nz
    width = (LAYERS // groups) * 2 * LANES
    vmem = pl.BlockSpec(memory_space=pltpu.VMEM)
    hbm = pl.BlockSpec(memory_space=pltpu.HBM)
    wide = width + LANES
    cutoffs = jnp.transpose(threshold, (0, 2, 1))
    held = [
        pltpu.with_memory_space_constraint(array, pltpu.HBM)
        for array in (kernels, observed, initial, cutoffs)
    ]
    coefficients, residual = pl.pallas_call(
        functools.partial(kernel, sizes),
        out_shape=(
            jax.ShapeDtypeStruct(initial.shape, BF16),
            jax.ShapeDtypeStruct(observed.shape, F32),
        ),
        in_specs=[hbm] * 4,
        out_specs=(vmem, vmem),
        scratch_shapes=[
            pltpu.VMEM(kernels.shape, BF16),
            pltpu.VMEM(observed.shape, F32),
            pltpu.VMEM(initial.shape, F32),
            pltpu.VMEM(cutoffs.shape, F32),
            pltpu.VMEM((8, LANES), F32),
            pltpu.VMEM((2, 8, LANES), F32),
            pltpu.VMEM((LAYERS * SLOTS, LANES), F32),
            pltpu.VMEM((LAYERS * SLOTS, LANES), BF16),
            pltpu.VMEM((2, LAYERS * SLOTS, LANES), BF16),
            pltpu.VMEM(initial.shape, BF16),
            pltpu.VMEM((8, LANES), F32),
            pltpu.VMEM((2, 4, LANES), F32),
            pltpu.VMEM((2, nv, 4, LANES), F32),
            pltpu.VMEM((2, groups, 8, wide), BF16),
            pltpu.VMEM((2, groups - 1, 8, wide), BF16),
            pltpu.VMEM((2, 8, wide), BF16),
            pltpu.VMEM((2, ny, 8, wide), BF16),
            pltpu.VMEM((groups, 8, width), BF16),
            pltpu.VMEM((groups, 8, width), BF16),
            pltpu.SemaphoreType.DMA((4,)),
            pltpu.SemaphoreType.DMA((10,)),
            pltpu.SemaphoreType.DMA((10,)),
            pltpu.SemaphoreType.REGULAR,
        ],
        compiler_params=pltpu.CompilerParams(
            collective_id=0, has_side_effects=True, vmem_limit_bytes=8 << 20
        ),
    )(*held)
    return pl.pallas_call(
        finish,
        out_shape=(
            jax.ShapeDtypeStruct(initial.shape, F32),
            jax.ShapeDtypeStruct(observed.shape, F32),
        ),
        in_specs=[vmem] * 2,
        out_specs=(vmem, vmem),
        compiler_params=pltpu.CompilerParams(vmem_limit_bytes=8 << 20),
    )(coefficients, residual)


def build(mesh, sizes):
    return jax.shard_map(
        functools.partial(body, sizes),
        mesh=mesh,
        in_specs=(P("dp", "vox"), P(None, "dp"), P(None, "vox"), P()),
        out_specs=(P(None, "vox"), P(None, "dp")),
        check_vma=False,
    )


def solution(mesh):
    return build(mesh, (NC, NY, NZ, NX, NH))
```

```python
import functools

import jax
import jax.numpy as jnp
from jax import lax
from jax.experimental import pallas as pl
from jax.experimental.pallas import tpu as pltpu
from jax.sharding import PartitionSpec as P

MESH = pl.DeviceIdType.MESH
F32 = jnp.float32
BF16 = jnp.bfloat16
LANES = 128
LAYERS = 16
SLOTS = 8

NC, NY, NZ, NX, NH = 2, 8, 4, 4, 4


def lane_of(rows=8):
    return lax.broadcasted_iota(jnp.int32, (rows, LANES), 1)


def shrink(values, cutoff):
    return jnp.where(
        values > cutoff, values - cutoff, jnp.where(values < -cutoff, values + cutoff, 0.0)
    )


def take_prev(tile, edge):
    return jnp.where(lane_of() == 0, edge, pltpu.roll(tile, 1, 1))


def take_next(tile, edge):
    return jnp.where(lane_of() == LANES - 1, edge, pltpu.roll(tile, LANES - 1, 1))


def inverse_wave(smooth, detail, detail_before, smooth_after, detail_after):
    even = smooth - 0.25 * (take_prev(detail, detail_before) + detail)
    even_after = smooth_after - 0.25 * (detail[:, LANES - 1 :] + detail_after)
    odd = detail + 0.5 * (even + take_next(even, even_after))
    return even, odd


def rows_dot(a, b):
    return lax.dot_general(a, b, (((1,), (1,)), ((), ())), preferred_element_type=F32)


def kernel(
    sizes,
    k_hbm,
    obs_hbm,
    init_hbm,
    thr_hbm,
    coef_ref,
    resid_ref,
    k_ref,
    obs_ref,
    init_ref,
    thr_ref,
    pack,
    packs,
    edge_f32,
    edge,
    edge_half,
    edges,
    model,
    pred_pad,
    pred_send,
    preds,
    stage,
    parts,
    sums_send,
    sums,
    chunks,
    finals,
    load_sem,
    send_sem,
    recv_sem,
    beyond_sem,
):
    nc, ny, nz, nx, nh = sizes
    nv = nx * nh
    groups = nc * nz
    per = LAYERS // groups
    width = per * 2 * LANES
    rows = k_ref.shape[0]
    dp = lax.axis_index("dp")
    vox = lax.axis_index("vox")
    core = lax.rem(dp, nc)
    y = lax.rem(lax.div(dp, nc), ny)
    z = lax.div(dp, nc * ny)
    g = z * nc + core

    loads = [
        pltpu.make_async_copy(init_hbm, init_ref, load_sem.at[0]),
        pltpu.make_async_copy(k_hbm, k_ref, load_sem.at[1]),
        pltpu.make_async_copy(obs_hbm, obs_ref, load_sem.at[2]),
        pltpu.make_async_copy(thr_hbm, thr_ref, load_sem.at[3]),
    ]
    for load in loads:
        load.start()

    x = lax.rem(vox, nx)
    high = lax.div(vox, nx)

    def curve_peer(k):
        return dp, lax.rem(vox + k, nv)

    def vox_peer(by):
        dh, dx = by
        return dp, lax.rem(high + dh, nh) * nx + lax.rem(x + dx, nx)

    group_order = []
    if nz == 4:
        group_order += [(nz - 1 - z, c) for c in range(nc)]
        group_order += [(lax.rem(z + 2, nz), c) for c in range(nc)]
    group_order += [(z + 1 - 2 * lax.rem(z, 2), c) for c in range(nc)]
    group_order += [(z, c) for c in range(1, nc)]
    group_order = [(oz, lax.rem(core + c, nc)) for oz, c in group_order]
    group_order = [(oz * nc + oc, (oz * ny + y) * nc + oc) for oz, oc in group_order]

    def y_peer(k):
        return (z * ny + lax.rem(y + k, ny)) * nc + core, vox

    vox_order = sorted(
        ((dh, dx) for dh in range(nh) for dx in range(nx) if dh or dx),
        key=lambda by: -(nz * min(by[0], nh - by[0]) + min(by[1], nx - by[1])),
    )
    near = [by for by in vox_order if min(by[0], nh - by[0]) < 2]
    y_order = sorted(range(1, ny), key=lambda k: -min(k, ny - k))

    barrier = pltpu.get_barrier_semaphore()

    def greet(peer, k):
        pl.semaphore_signal(barrier, inc=1, device_id=peer(k), device_id_type=MESH)

    for k in y_order:
        greet(y_peer, k)
    for by in near:
        greet(vox_peer, by)
    for _, other in group_order:
        pl.semaphore_signal(
            barrier, inc=1, device_id=(other, vox), device_id_type=MESH
        )

    def send(src, dst, phase, device):
        pltpu.make_async_remote_copy(
            src_ref=src,
            dst_ref=dst,
            send_sem=send_sem.at[phase],
            recv_sem=recv_sem.at[phase],
            device_id=device,
            device_id_type=MESH,
        ).start()

    def wait(ref, sem, phase):
        pltpu.make_async_copy(ref, ref, sem.at[phase]).wait()

    def turn(tile, by):
        by = by % LANES
        return pltpu.roll(tile, by, 1) if by else tile

    lane = lane_of()
    slot = lax.rem(lane, SLOTS)
    loads[0].wait()
    packed = jnp.zeros((8, LANES), F32)
    for layer in range(LAYERS):
        base = layer * 2 * LANES
        smooth = init_ref[:, base : base + LANES]
        detail = init_ref[:, base + LANES : base + 2 * LANES]
        at = layer * SLOTS
        packed = jnp.where(lane == at, turn(smooth, at), packed)
        packed = jnp.where(lane == at + 1, turn(detail, at + 1), packed)
        packed = jnp.where(lane == at + 4, turn(detail, at + 5), packed)
    pack[...] = packed

    pl.semaphore_wait(barrier, len(near) + (groups - 1) + (ny - 1))
    pl.semaphore_signal(
        beyond_sem, inc=1, device_id=vox_peer((nh - 1, 0)), device_id_type=MESH
    )

    send(pack, packs.at[0], 0, curve_peer(nv - 1))
    send(pack, packs.at[1], 0, curve_peer(1))

    loads[1].wait()
    pick_slot = lax.broadcasted_iota(jnp.int32, (SLOTS, 2 * LANES), 0)
    column = lax.broadcasted_iota(jnp.int32, (SLOTS, 2 * LANES), 1)
    picked = (
        ((pick_slot == 0) & (column == 0))
        | ((pick_slot == 1) & (column == LANES))
        | ((pick_slot == 2) & (column == 1))
        | ((pick_slot == 3) & (column == LANES - 1))
        | ((pick_slot == 4) & (column == 2 * LANES - 1))
    )
    pick = jnp.where(picked, 1.0, 0.0).astype(BF16)
    edge_f32[...] = jnp.zeros_like(edge_f32)
    pred_pad[...] = jnp.zeros_like(pred_pad)
    for layer in range(LAYERS):
        base = layer * 2 * LANES
        edge_f32[layer * SLOTS : (layer + 1) * SLOTS, 0:rows] = rows_dot(
            pick, k_ref[:, base : base + 2 * LANES]
        )
    edge[...] = edge_f32[...].astype(BF16)
    half = LAYERS * SLOTS // 2
    edge_half[...] = (
        edge_f32[0:half, :] + pltpu.roll(edge_f32[half:, :], LANES // 2, 1)
    ).astype(BF16)

    inner = jnp.zeros((8, LANES), F32)
    for layer in range(LAYERS):
        base = layer * 2 * LANES
        at = layer * SLOTS
        smooth = init_ref[:, base : base + LANES]
        detail = init_ref[:, base + LANES : base + 2 * LANES]
        even = smooth - 0.25 * (turn(detail, 1) + detail)
        odd = detail + 0.5 * (even + turn(even, -1))
        inner = jnp.where(lane == at + 1, turn(even, at), inner)
        inner = jnp.where(lane == at + 4, turn(even, at + 5), inner)
        even = jnp.where(lane == 0, 0.0, even)
        odd = jnp.where((lane == 0) | (lane == LANES - 1), 0.0, odd)
        model[:, base : base + LANES] = even.astype(BF16)
        model[:, base + LANES : base + 2 * LANES] = odd.astype(BF16)
    pred_pad[:, 0:rows] = rows_dot(model[...], k_ref[...])
    pred_inner = pred_pad[...]
    detail_first = turn(packed, -1)

    wait(packs, recv_sem, 0)
    after = packs[0]
    before = packs[1]
    even_first = packed - 0.25 * (turn(before, -4) + detail_first)
    odd_first = packed + 0.5 * (turn(even_first, 1) + inner)
    even_after = turn(after, 4) - 0.25 * (packed + turn(after, 3))
    odd_last = packed + 0.5 * (inner + even_after)
    rim = jnp.where(
        slot == 0,
        even_first,
        jnp.where(slot == 1, odd_first, jnp.where(slot == 4, odd_last, 0.0)),
    )
    padded = pred_inner + jnp.dot(rim.astype(BF16), edge[...], preferred_element_type=F32)

    state = []
    for it in range(2):
        phase = 2 + 4 * it
        shared = padded[0:4] + pltpu.roll(padded[4:8], rows, 1)
        pred_send[it] = shared
        preds[it, vox] = shared
        if it == 0:
            pl.semaphore_wait(beyond_sem, 1)
        for by in vox_order:
            send(pred_send.at[it], preds.at[it, vox], phase, vox_peer(by))

        if it == 0:
            send(edge_half, edges.at[0], 1, curve_peer(nv - 1))
            send(edge_half, edges.at[1], 1, curve_peer(1))
            loads[2].wait()
            loads[3].wait()
            mine = pl.ds(pl.multiple_of(g * width, width), width)
            back = lax.rem(LANES - g * (per * SLOTS), LANES)
            after = pltpu.roll(after, back, 1)
            before = pltpu.roll(before, back, 1)
            pred_pad[:, 64:80] = thr_ref[:, 0, :]
            pred_pad[:, 96:112] = thr_ref[:, 1, :]
            cutoffs = pltpu.roll(pred_pad[...], lax.rem(LANES - g * per, LANES), 1)
            own = init_ref[:, mine]
            cuts = []
            for i in range(per):
                base = i * 2 * LANES
                at = i * SLOTS
                cuts.append(
                    tuple(
                        jnp.broadcast_to(cutoffs[:, c + i : c + i + 1], (8, LANES))
                        for c in (64, 96)
                    )
                )
                state.append(
                    (
                        own[:, base : base + LANES],
                        own[:, base + LANES : base + 2 * LANES],
                        before[:, at + 4 : at + 5],
                        after[:, at : at + 1],
                        after[:, at + 1 : at + 2],
                    )
                )
            wait(edges, recv_sem, 1)
            place = lax.rem(
                lax.broadcasted_iota(jnp.int32, (half, LANES), 0), SLOTS
            )
            halves = jnp.where(
                place < 3, edges[0].astype(F32), edges[1].astype(F32)
            )
            edge_f32[0:half, :] = halves
            edge_f32[half:, :] = pltpu.roll(halves, LANES // 2, 1)
            beyond = edge_f32[:, 0:rows].astype(BF16)

        wait(preds.at[it, pl.ds(0, nv - 1)], recv_sem, phase)
        total = preds[it, 0]
        for j in range(1, nv):
            total = total + preds[it, j]
        predicted = jnp.concatenate(
            [total[:, 0:rows], pltpu.roll(total, LANES - rows, 1)[:, 0:rows]], axis=0
        )
        residual = obs_ref[...] - predicted
        sent = residual.astype(BF16)

        grad = jnp.dot(sent, k_ref[...], preferred_element_type=F32).astype(BF16)
        edge_grad = rows_dot(sent, beyond).astype(BF16)
        for i in range(groups):
            stage[it, i, :, 0:width] = grad[:, i * width : (i + 1) * width]
            stage[it, i, :, width:] = edge_grad

        for i, (chunk, other) in enumerate(group_order):
            send(stage.at[it, chunk], parts.at[it, i], phase + 1, (other, vox))
        if it == 1:
            resid_ref[...] = residual
        wait(parts.at[it], recv_sem, phase + 1)
        total = stage[it, g].astype(F32)
        for i in range(groups - 1):
            total = total + parts[it, i].astype(F32)
        total = total.astype(BF16)
        sums_send[it] = total
        sums[it, y] = total
        for k in y_order:
            send(sums_send.at[it], sums.at[it, y], phase + 2, y_peer(k))
        wait(sums.at[it, pl.ds(0, ny - 1)], recv_sem, phase + 2)
        total = sums[it, 0].astype(F32)
        for i in range(1, ny):
            total = total + sums[it, i].astype(F32)
        beside = pltpu.roll(total[:, width:], back, 1)

        for i in range(per):
            base = i * 2 * LANES
            at = i * SLOTS
            even = total[:, base : base + LANES]
            odd = total[:, base + LANES : base + 2 * LANES]
            even_after = beside[:, at : at + 1]
            odd_after = beside[:, at + 1 : at + 2]
            even_after2 = beside[:, at + 2 : at + 3]
            even_before = beside[:, at + 3 : at + 4]
            odd_before = beside[:, at + 4 : at + 5]
            detail = odd - 0.5 * (even + take_next(even, even_after))
            detail_before = odd_before - 0.5 * (even_before + even[:, 0:1])
            smooth = even + 0.25 * (take_prev(detail, detail_before) + detail)
            cut_s, cut_d = cuts[i]
            w_s, w_d, w_db, w_sa, w_da = state[i]
            w_s = shrink(w_s + 0.5 * smooth, cut_s)
            w_d = shrink(w_d + 0.5 * detail, cut_d)
            if it == 0:
                detail_after = odd_after - 0.5 * (even_after + even_after2)
                smooth_after = even_after + 0.25 * (detail[:, LANES - 1 :] + detail_after)
                w_db = shrink(w_db + 0.5 * detail_before, cut_d[:, 0:1])
                w_sa = shrink(w_sa + 0.5 * smooth_after, cut_s[:, 0:1])
                w_da = shrink(w_da + 0.5 * detail_after, cut_d[:, 0:1])
                state[i] = (w_s, w_d, w_db, w_sa, w_da)
                w_s, w_d = inverse_wave(w_s, w_d, w_db, w_sa, w_da)
            target = chunks if it == 0 else finals
            target[g, :, base : base + LANES] = w_s.astype(BF16)
            target[g, :, base + LANES : base + 2 * LANES] = w_d.astype(BF16)

        for _, other in group_order:
            send(target.at[g], target.at[g], phase + 3, (other, vox))
        wait(target.at[pl.ds(0, groups - 1)], recv_sem, phase + 3)
        if it == 0:
            pred = rows_dot(chunks[0], k_ref[:, 0:width])
            for i in range(1, groups):
                pred = pred + rows_dot(chunks[i], k_ref[:, i * width : (i + 1) * width])
            pred_pad[...] = jnp.zeros_like(pred_pad)
            pred_pad[:, 0:rows] = pred
            padded = pred_pad[...]
        else:
            for i in range(groups):
                coef_ref[:, i * width : (i + 1) * width] = finals[i]

    wait(packs, send_sem, 0)
    wait(edges, send_sem, 1)
    for it in range(2):
        phase = 2 + 4 * it
        target = chunks if it == 0 else finals
        wait(preds.at[it, pl.ds(0, nv - 1)], send_sem, phase)
        wait(parts.at[it], send_sem, phase + 1)
        wait(sums.at[it, pl.ds(0, ny - 1)], send_sem, phase + 2)
        wait(target.at[pl.ds(0, groups - 1)], send_sem, phase + 3)


def finish(narrow_ref, held_ref, coef_ref, resid_ref):
    coef_ref[...] = narrow_ref[...].astype(F32)
    resid_ref[...] = held_ref[...]


def body(sizes, kernels, observed, initial, threshold):
    nc, ny, nz, nx, nh = sizes
    nv = nx * nh
    groups = nc * nz
    width = (LAYERS // groups) * 2 * LANES
    vmem = pl.BlockSpec(memory_space=pltpu.VMEM)
    hbm = pl.BlockSpec(memory_space=pltpu.HBM)
    wide = width + LANES
    cutoffs = jnp.transpose(threshold, (0, 2, 1))
    held = [
        pltpu.with_memory_space_constraint(array, pltpu.HBM)
        for array in (kernels, observed, initial, cutoffs)
    ]
    coefficients, residual = pl.pallas_call(
        functools.partial(kernel, sizes),
        out_shape=(
            jax.ShapeDtypeStruct(initial.shape, BF16),
            jax.ShapeDtypeStruct(observed.shape, F32),
        ),
        in_specs=[hbm] * 4,
        out_specs=(vmem, vmem),
        scratch_shapes=[
            pltpu.VMEM(kernels.shape, BF16),
            pltpu.VMEM(observed.shape, F32),
            pltpu.VMEM(initial.shape, F32),
            pltpu.VMEM(cutoffs.shape, F32),
            pltpu.VMEM((8, LANES), F32),
            pltpu.VMEM((2, 8, LANES), F32),
            pltpu.VMEM((LAYERS * SLOTS, LANES), F32),
            pltpu.VMEM((LAYERS * SLOTS, LANES), BF16),
            pltpu.VMEM((LAYERS * SLOTS // 2, LANES), BF16),
            pltpu.VMEM((2, LAYERS * SLOTS // 2, LANES), BF16),
            pltpu.VMEM(initial.shape, BF16),
            pltpu.VMEM((8, LANES), F32),
            pltpu.VMEM((2, 4, LANES), F32),
            pltpu.VMEM((2, nv, 4, LANES), F32),
            pltpu.VMEM((2, groups, 8, wide), BF16),
            pltpu.VMEM((2, groups - 1, 8, wide), BF16),
            pltpu.VMEM((2, 8, wide), BF16),
            pltpu.VMEM((2, ny, 8, wide), BF16),
            pltpu.VMEM((groups, 8, width), BF16),
            pltpu.VMEM((groups, 8, width), BF16),
            pltpu.SemaphoreType.DMA((4,)),
            pltpu.SemaphoreType.DMA((10,)),
            pltpu.SemaphoreType.DMA((10,)),
            pltpu.SemaphoreType.REGULAR,
        ],
        compiler_params=pltpu.CompilerParams(
            collective_id=0, has_side_effects=True, vmem_limit_bytes=8 << 20
        ),
    )(*held)
    return pl.pallas_call(
        finish,
        out_shape=(
            jax.ShapeDtypeStruct(initial.shape, F32),
            jax.ShapeDtypeStruct(observed.shape, F32),
        ),
        in_specs=[vmem] * 2,
        out_specs=(vmem, vmem),
        compiler_params=pltpu.CompilerParams(vmem_limit_bytes=8 << 20),
    )(coefficients, residual)


def build(mesh, sizes):
    return jax.shard_map(
        functools.partial(body, sizes),
        mesh=mesh,
        in_specs=(P("dp", "vox"), P(None, "dp"), P(None, "vox"), P()),
        out_specs=(P(None, "vox"), P(None, "dp")),
        check_vma=False,
    )


def solution(mesh):
    return build(mesh, (NC, NY, NZ, NX, NH))
```
